32 devices in a mesh: tok: 16 (over z, y, x), col: 2 (over core).
Axes of the slice: x: 2, y: 2, z: 4, core: 2. Of those that a mesh axis runs over, the one named last changes fastest.
Arguments:
- activations: bfloat16 [512, 6144], P('tok', 'col'), may hold values from -61 to 61
- block_slot: int32 [6], replicated, may hold values from 0 to 5, each once
- slot_tile: int32 [32], replicated, may hold values from 0 to 31, each once
Outputs:
- gram_tiles: float32 [32, 1024, 1024], P(('tok', 'col'))
- col_mean: float32 [6144], P('col')
- col_var: float32 [6144], P('col')
The draws below stay inside these ranges and needn't reach their ends.
Inputs may be any that keep to these rules, and one draw needn't show every extreme that they name: `block_slot`: each stored position once. `slot_tile`: each value once.
All inputs are finite; a program needn't handle non-finite values.
Results may differ from the reference program's by a relative error of at most 0.0003.
Values may be sent and summed in bfloat16 or wider, within the bound.
No kernel may reach another device: no remote copies, remote signals or barrier semaphores. Data moves between devices by JAX's collectives and lax.ppermute only.
A program may use at most 64 MiB of HBM per device.

```python
import math
import jax
import jax.numpy as jnp
import numpy as np
from jax import lax

BS = 1024
NB = 6
F = 6144
TOKENS = 512
DEVICES = 32


def draw_activations(key, part):
    keys = jax.random.split(jax.random.fold_in(key, 11), 5)
    col_scale = jnp.exp(jax.random.uniform(keys[0], (F,), jnp.float32, -1.2, 1.2))
    position = jnp.arange(TOKENS, dtype=jnp.float32)[:, None] / TOKENS
    tok_scale = jnp.exp(math.log(3.0) * position + jax.random.uniform(keys[1], (TOKENS, 1), jnp.float32, -0.3, 0.3))
    offset = jax.random.uniform(keys[2], (F,), jnp.float32, -0.5, 0.5)
    noise = jnp.clip(jax.random.normal(keys[4], (TOKENS, F), jnp.float32), -4.0, 4.0)
    return ((offset + noise) * col_scale * tok_scale).astype(jnp.bfloat16)


def setup_inputs(seed: int = 0) -> dict:
    key_list = jax.random.split(jax.random.key(seed), 4)
    return {
        "activations": draw_activations(jax.random.fold_in(key_list[3], 71), 0),
        "block_slot": jax.random.permutation(key_list[1], NB).astype(jnp.int32),
        "slot_tile": jax.random.permutation(key_list[2], DEVICES).astype(jnp.int32),
    }


def reference(activations, block_slot, slot_tile):
    block_count = F // BS
    pair_count = block_count * (block_count + 1) // 2
    rows_np, cols_np = np.triu_indices(block_count)
    row_table = jnp.asarray(rows_np.astype(np.int32))
    col_table = jnp.asarray(cols_np.astype(np.int32))
    blocks = activations.reshape(TOKENS, block_count, BS)
    values = activations.astype(jnp.float32)
    col_mean = jnp.sum(values, axis=0) / TOKENS
    col_var = jnp.sum((values - col_mean) ** 2, axis=0) / TOKENS

    def one_slot(tile_index):
        usable = tile_index < pair_count
        clamped = jnp.where(usable, tile_index, 0).astype(jnp.int32)
        first_slot = block_slot[row_table[clamped]].astype(jnp.int32)
        second_slot = block_slot[col_table[clamped]].astype(jnp.int32)
        left_block = lax.dynamic_index_in_dim(blocks, first_slot, 1, keepdims=False)
        right_block = lax.dynamic_index_in_dim(blocks, second_slot, 1, keepdims=False)
        product = jnp.dot(left_block.T, right_block, preferred_element_type=jnp.float32) / TOKENS
        return jnp.where(usable, product, jnp.zeros_like(product))

    gram_tiles = lax.map(one_slot, slot_tile)
    return (gram_tiles, col_mean, col_var)
```

```python
import jax
import jax.numpy as jnp
import numpy as np
from jax import lax
from jax.experimental import pallas as pl
from jax.experimental.pallas import tpu as pltpu
from jax.sharding import PartitionSpec as P

BS = 1024


def split_tok(n_tok):
    n_in = 1
    while n_in * n_in < n_tok:
        n_in *= 2
    return n_tok // n_in, n_in


def outer_waves(n_out):
    waves = [[0]]
    for k in range(1, n_out // 2 + 1):
        waves.append([k] if 2 * k == n_out else [k, n_out - k])
    return waves


def pair_of(tile, block_count):
    pair_count = block_count * (block_count + 1) // 2
    tile = jnp.where(tile < pair_count, tile, 0)
    row = jnp.int32(0)
    start = jnp.int32(0)
    for r in range(1, block_count):
        first = r * block_count - r * (r - 1) // 2
        beyond = tile >= first
        row = jnp.where(beyond, r, row)
        start = jnp.where(beyond, first, start)
    return row, tile - start + row


def select_kernel(n_in, n_col, block_count, n_shards, *refs):
    slot_ref, tile_ref = refs[0], refs[1]
    shards = refs[2 : 2 + n_shards * n_col]
    outs = refs[2 + n_shards * n_col :]
    tok_dev, width = shards[0].shape
    held = width // BS
    tok = lax.axis_index("tok")
    col = lax.axis_index("col")
    inner = lax.rem(tok, n_in)
    for k in range(n_in):
        peer = tok - inner + (inner ^ k)
        pair = pair_of(tile_ref[peer * n_col + col], block_count)
        for side in range(2):
            block = slot_ref[pair[side]]
            owner = lax.div(block, held)
            column = pl.multiple_of((block - owner * held) * BS, BS)
            away = lax.rem(owner - col + n_col, n_col)
            for r in range(n_col):

                @pl.when(away == r)
                def _():
                    for s in range(n_shards):
                        outs[k][s * tok_dev : (s + 1) * tok_dev, side * BS : (side + 1) * BS] = (
                            shards[s * n_col + r][:, pl.ds(column, BS)]
                        )


def select(n_in, n_col, block_count, block_slot, slot_tile, shards):
    rows = len(shards) * shards[0][0].shape[0]
    smem = pl.BlockSpec(memory_space=pltpu.SMEM)
    vmem = pl.BlockSpec(memory_space=pltpu.VMEM)
    flat = [a for shard in shards for a in shard]
    return pl.pallas_call(
        lambda *refs: select_kernel(n_in, n_col, block_count, len(shards), *refs),
        out_shape=[jax.ShapeDtypeStruct((rows, 2 * BS), jnp.bfloat16)] * n_in,
        in_specs=[smem, smem] + [vmem] * len(flat),
        out_specs=[vmem] * n_in,
        name="select",
    )(block_slot, slot_tile, *flat)


def on_device(activations, block_slot, slot_tile):
    n_tok = lax.axis_size("tok")
    n_col = lax.axis_size("col")
    n_out, n_in = split_tok(n_tok)
    tok_dev, width = activations.shape
    total_tokens = tok_dev * n_tok
    block_count = width * n_col // BS
    pair_count = block_count * (block_count + 1) // 2

    def from_outer(a, k):
        pairs = [(t, (t // n_in + k) % n_out * n_in + t % n_in) for t in range(n_tok)]
        return lax.ppermute(a, "tok", pairs)

    def from_inner(a, k):
        return lax.ppermute(a, "tok", [(t, t ^ k) for t in range(n_tok)])

    def all_columns(a):
        return [a] + [
            lax.ppermute(a, "col", [(c, (c - r) % n_col) for c in range(n_col)])
            for r in range(1, n_col)
        ]

    shard = {0: activations}
    full = {0: all_columns(activations)}
    waves = outer_waves(n_out)
    for wave in waves[1:]:
        for k in wave:
            shard[k] = from_outer(activations, k)
    pieces = []
    for wave in waves:
        for k in wave:
            if k:
                full[k] = all_columns(shard[k])
        picked = select(n_in, n_col, block_count, block_slot, slot_tile, [full[k] for k in wave])
        pieces.append(picked[0])
        for k in range(1, n_in):
            pieces.append(from_inner(picked[k], k))

    def merge(a, b, count):
        return a[0] + b[0], a[1] + b[1] + (a[0] - b[0]) ** 2 / (2 * count)

    stats = []
    for k in range(n_out):
        values = shard[k].astype(jnp.float32)
        part = jnp.sum(values, axis=0)
        stats.append((part, jnp.sum((values - part / tok_dev) ** 2, axis=0)))
    count = tok_dev
    while len(stats) > 1:
        half = len(stats) // 2
        stats = [merge(stats[k], stats[k + half], count) for k in range(half)]
        count *= 2
    mine = stats[0]
    k = 1
    while k < n_in:
        other = from_inner(jnp.stack(mine), k)
        mine = merge(mine, (other[0], other[1]), count)
        count *= 2
        k *= 2
    col_mean = mine[0] / total_tokens
    col_var = mine[1] / total_tokens

    arrived = jnp.concatenate(pieces, axis=0)
    own_slot = lax.axis_index("tok") * n_col + lax.axis_index("col")
    own_tile = lax.dynamic_index_in_dim(slot_tile, own_slot, 0, keepdims=False)
    product = (
        lax.dot_general(
            arrived[:, :BS],
            arrived[:, BS:],
            (((0,), (0,)), ((), ())),
            preferred_element_type=jnp.float32,
        )
        / total_tokens
    )
    product = jnp.where(own_tile < pair_count, product, jnp.zeros_like(product))
    return (product[None], col_mean, col_var)


def solution(mesh):
    return jax.shard_map(
        on_device,
        mesh=mesh,
        in_specs=(P("tok", "col"), P(), P()),
        out_specs=(P(("tok", "col"), None, None), P("col"), P("col")),
        check_vma=False,
    )
```

```python
import jax
import jax.numpy as jnp
import numpy as np
from jax import lax
from jax.experimental import pallas as pl
from jax.experimental.pallas import tpu as pltpu
from jax.sharding import PartitionSpec as P

BS = 1024


def split_tok(n_tok):
    n_in = 1
    while n_in * n_in < n_tok:
        n_in *= 2
    return n_tok // n_in, n_in


def outer_waves(n_out):
    waves = [[0], [1, 2], [3]] if n_out >= 4 else [[k] for k in range(n_out)]
    return waves + [[k, k + 1] for k in range(4, n_out, 2)]


def pair_of(tile, block_count):
    pair_count = block_count * (block_count + 1) // 2
    tile = jnp.where(tile < pair_count, tile, 0)
    row = jnp.int32(0)
    start = jnp.int32(0)
    for r in range(1, block_count):
        first = r * block_count - r * (r - 1) // 2
        beyond = tile >= first
        row = jnp.where(beyond, r, row)
        start = jnp.where(beyond, first, start)
    return row, tile - start + row


def select_kernel(n_in, n_col, block_count, n_shards, *refs):
    slot_ref, tile_ref = refs[0], refs[1]
    shards = refs[2 : 2 + n_shards * n_col]
    outs = refs[2 + n_shards * n_col :]
    tok_dev, width = shards[0].shape
    held = width // BS
    tok = lax.axis_index("tok")
    col = lax.axis_index("col")
    inner = lax.rem(tok, n_in)
    for k in range(n_in):
        peer = tok - inner + (inner ^ k)
        pair = pair_of(tile_ref[peer * n_col + col], block_count)
        for side in range(2):
            block = slot_ref[pair[side]]
            owner = lax.div(block, held)
            column = pl.multiple_of((block - owner * held) * BS, BS)
            away = lax.rem(owner - col + n_col, n_col)
            for r in range(n_col):

                @pl.when(away == r)
                def _():
                    for s in range(n_shards):
                        outs[k][s * tok_dev : (s + 1) * tok_dev, side * BS : (side + 1) * BS] = (
                            shards[s * n_col + r][:, pl.ds(column, BS)]
                        )


def select(n_in, n_col, block_count, block_slot, slot_tile, shards, near):
    rows = len(shards) * shards[0][0].shape[0]
    flat = [near.put(a) for shard in shards for a in shard]
    return pl.pallas_call(
        lambda *refs: select_kernel(n_in, n_col, block_count, len(shards), *refs),
        out_shape=[near.out((rows, 2 * BS), jnp.bfloat16)] * n_in,
        in_specs=[SMEM, SMEM] + [VMEM] * len(flat),
        out_specs=[VMEM] * n_in,
        cost_estimate=pl.CostEstimate(flops=0, transcendentals=0, bytes_accessed=8 * rows * 2 * BS),
        name="select",
    )(block_slot, slot_tile, *flat)


def merge(a, b, count):
    return a[0] + b[0], a[1] + b[1] + (a[0] - b[0]) ** 2 / (2 * count)


def stats_kernel(*refs):
    shards, out = refs[:-1], refs[-1]
    count = shards[0].shape[0]
    parts = []
    for ref in shards:
        values = ref[...].astype(jnp.float32)
        part = jnp.sum(values, axis=0, keepdims=True)
        parts.append((part, jnp.sum((values - part / count) ** 2, axis=0, keepdims=True)))
    while len(parts) > 1:
        half = len(parts) // 2
        parts = [merge(parts[k], parts[k + half], count) for k in range(half)]
        count *= 2
    out[0:1, :] = parts[0][0]
    out[1:2, :] = parts[0][1]


def local_stats(shards, near):
    tok_dev, width = shards[0].shape
    return pl.pallas_call(
        stats_kernel,
        out_shape=near.out((2, width), jnp.float32),
        in_specs=[VMEM] * len(shards),
        out_specs=VMEM,
        cost_estimate=pl.CostEstimate(
            flops=4 * len(shards) * tok_dev * width,
            transcendentals=0,
            bytes_accessed=2 * len(shards) * tok_dev * width,
        ),
        name="stats",
    )(*[near.put(a) for a in shards])


def gram_kernel(n_col, pair_count, tile_ref, *refs):
    pieces, (out, left, right, chunk, sems) = refs[:-5], refs[-5:]
    total_tokens = left.shape[0]
    start = 0
    for ref in pieces:
        rows = ref.shape[0]
        left[start : start + rows, :] = ref[:, :BS]
        right[start : start + rows, :] = ref[:, BS:]
        start += rows
    mine = tile_ref[lax.axis_index("tok") * n_col + lax.axis_index("col")]
    rows = chunk.shape[1]
    copies = [None, None]
    for m in range(BS // rows):
        slot = m % 2
        if copies[slot] is not None:
            copies[slot].wait()
        product = lax.dot_general(
            left[:, m * rows : (m + 1) * rows],
            right[...],
            (((0,), (0,)), ((), ())),
            preferred_element_type=jnp.float32,
        )
        chunk[slot] = jnp.where(mine < pair_count, product / total_tokens, 0.0)
        copies[slot] = pltpu.make_async_copy(
            chunk.at[slot], out.at[0, m * rows : (m + 1) * rows, :], sems.at[slot]
        )
        copies[slot].start()
    for copy in copies:
        copy.wait()


def gram(n_col, pair_count, slot_tile, pieces, near):
    total_tokens = sum(a.shape[0] for a in pieces)
    return pl.pallas_call(
        lambda *refs: gram_kernel(n_col, pair_count, *refs),
        out_shape=jax.ShapeDtypeStruct((1, BS, BS), jnp.float32),
        in_specs=[SMEM] + [VMEM] * len(pieces),
        out_specs=pl.BlockSpec(memory_space=pl.ANY),
        scratch_shapes=[
            pltpu.VMEM((total_tokens, BS), jnp.bfloat16),
            pltpu.VMEM((total_tokens, BS), jnp.bfloat16),
            pltpu.VMEM((2, BS // 4, BS), jnp.float32),
            pltpu.SemaphoreType.DMA((2,)),
        ],
        cost_estimate=pl.CostEstimate(
            flops=2 * total_tokens * BS * BS, transcendentals=0, bytes_accessed=4 * BS * BS
        ),
        name="gram",
    )(slot_tile, *[near.put(a) for a in pieces])


SMEM = pl.BlockSpec(memory_space=pltpu.SMEM)
VMEM = pl.BlockSpec(memory_space=pltpu.VMEM)


class Near:
    def __init__(self, fits):
        self.fits = fits

    def put(self, a):
        return pltpu.with_memory_space_constraint(a, pltpu.VMEM) if self.fits else a

    def out(self, shape, dtype):
        return pltpu.VMEM(shape, dtype) if self.fits else jax.ShapeDtypeStruct(shape, dtype)


def after(value, *earlier):
    return lax.optimization_barrier((value, *earlier))[0]


def by_blocks(activations, block_slot, slot_tile):
    n_tok = lax.axis_size("tok")
    n_col = lax.axis_size("col")
    n_out, n_in = split_tok(n_tok)
    tok_dev, width = activations.shape
    total_tokens = tok_dev * n_tok
    block_count = width * n_col // BS
    pair_count = block_count * (block_count + 1) // 2
    held = 2 * tok_dev * (n_out * n_col * width + 2 * n_tok * 2 * BS)
    near = Near(held <= 12 << 20)

    def from_outer(a, k):
        return lax.ppermute(a, "tok", [(t, t ^ (k * n_in)) for t in range(n_tok)])

    def from_inner(a, k):
        return lax.ppermute(a, "tok", [(t, t ^ k) for t in range(n_tok)])

    def all_columns(a):
        return [a] + [
            lax.ppermute(a, "col", [(c, (c - r) % n_col) for c in range(n_col)])
            for r in range(1, n_col)
        ]

    waves = outer_waves(n_out)
    shard = {0: activations}
    source = activations
    pieces = []
    done = None
    for w, wave in enumerate(waves):
        full = []
        for k in wave:
            if k:
                shard[k] = after(from_outer(activations if w < 2 else source, k), done)
            full.append(all_columns(shard[k]))
        source = after(activations, *[shard[k] for k in wave if k])
        picked = select(n_in, n_col, block_count, block_slot, slot_tile, full, near)
        if pieces:
            picked = lax.optimization_barrier((*picked, *arrived))[:n_in]
        done = picked[0]
        pieces.append(picked[0])
        arrived = [from_inner(picked[k], k) for k in range(1, n_in)]
        pieces.extend(arrived)

    mine = local_stats([after(shard[k], done) for k in range(n_out)], near)
    mine = (mine[0], mine[1])
    count = tok_dev * n_out
    k = 1
    while k < n_in:
        other = from_inner(jnp.stack(mine), k)
        mine = merge(mine, (other[0], other[1]), count)
        count *= 2
        k *= 2
    product = gram(n_col, pair_count, slot_tile, pieces, near)
    return (product, mine[0] / total_tokens, mine[1] / total_tokens)


def wanted(tile_ref, slot_ref, col, block_count, n_col):
    pair = pair_of(tile_ref[lax.axis_index("tok") * n_col + col], block_count)
    return slot_ref[pair[0]], slot_ref[pair[1]]


def stat_tree(parts, count):
    while len(parts) > 1:
        half = len(parts) // 2
        parts = [merge(parts[k], parts[k + half], count) for k in range(half)]
        count *= 2
    return parts[0]


def shard_stats(ref):
    values = ref[...].astype(jnp.float32)
    part = jnp.sum(values, axis=0, keepdims=True)
    mean = part / values.shape[0]
    return part, jnp.sum((values - mean) ** 2, axis=0, keepdims=True)


def take_block(block, col, held, pieces, starts, dst):
    owner = lax.div(block, held)
    column = pl.multiple_of((block - owner * held) * BS, BS)

    @pl.when(owner == col)
    def _():
        for ref, start in zip(pieces, starts):
            dst[pl.ds(start, ref.shape[0]), :] = ref[:, pl.ds(column, BS)]


def wave_kernel(block_count, slot_ref, tile_ref, *refs):
    shards, (own, other, stats) = refs[:-3], refs[-3:]
    tok_dev, width = shards[0].shape
    col = lax.axis_index("col")
    first = pl.multiple_of((1 + col) * tok_dev, tok_dev)
    second = pl.multiple_of((2 - col) * tok_dev, tok_dev)
    starts = (0, first, second, 3 * tok_dev)
    for out, target in ((own, col), (other, 1 - col)):
        for side, block in enumerate(wanted(tile_ref, slot_ref, target, block_count, 2)):
            side_out = out.at[:, side * BS : (side + 1) * BS]
            take_block(block, col, width // BS, shards, starts, side_out)
    parts = [shard_stats(ref) for ref in shards]
    if len(parts) == 4:
        parts = [stat_tree(parts, tok_dev)]
    else:
        parts = [merge(parts[0], parts[2], tok_dev), parts[1]]
    for k, (part, square) in enumerate(parts):
        stats[2 * k : 2 * k + 1, :] = part
        stats[2 * k + 1 : 2 * k + 2, :] = square


def wave_parts(block_count, block_slot, slot_tile, shards):
    tok_dev, width = shards[0].shape
    near = Near(True)
    rows = len(shards) * tok_dev
    return pl.pallas_call(
        lambda *refs: wave_kernel(block_count, *refs),
        out_shape=[
            near.out((rows, 2 * BS), jnp.bfloat16),
            near.out((rows, 2 * BS), jnp.bfloat16),
            near.out((2 if len(shards) == 4 else 4, width), jnp.float32),
        ],
        in_specs=[SMEM, SMEM] + [VMEM] * len(shards),
        out_specs=[VMEM] * 3,
        cost_estimate=pl.CostEstimate(flops=0, transcendentals=0, bytes_accessed=2 * rows * width),
        compiler_params=pltpu.CompilerParams(vmem_limit_bytes=4 << 20),
        name="wave",
    )(block_slot, slot_tile, *[near.put(a) for a in shards])


def assemble(blocks, col, held, own, other, sides, start):
    for side, block in enumerate(blocks):
        here = lax.div(block, held) == col
        for parts, taken in ((own, here), (other, jnp.logical_not(here))):

            @pl.when(taken)
            def _():
                row = start
                for ref in parts:
                    rows = ref.shape[0]
                    sides[side][row : row + rows, :] = ref[:, side * BS : (side + 1) * BS]
                    row += rows
    return start + sum(ref.shape[0] for ref in own)


def product_rows(left, right, m, rows):
    return lax.dot_general(
        left[:, m * rows : (m + 1) * rows],
        right[...],
        (((0,), (0,)), ((), ())),
        preferred_element_type=jnp.float32,
    )


def partial_kernel(block_count, held, slot_ref, tile_ref, *refs):
    parts, (acc, left, right) = refs[:-3], refs[-3:]
    half = len(parts) // 2
    col = lax.axis_index("col")
    blocks = wanted(tile_ref, slot_ref, col, block_count, 2)
    assemble(blocks, col, held, parts[:half], parts[half:], (left, right), 0)
    rows = BS // 4
    for m in range(BS // rows):
        acc[m * rows : (m + 1) * rows, :] = product_rows(left, right, m, rows)


def partial_gram(block_count, held, block_slot, slot_tile, own, other):
    near = Near(True)
    tokens = sum(a.shape[0] for a in own)
    arrays = [near.put(a) for a in (*own, *other)]
    return pl.pallas_call(
        lambda *refs: partial_kernel(block_count, held, *refs),
        out_shape=near.out((BS, BS), jnp.float32),
        in_specs=[SMEM, SMEM] + [VMEM] * len(arrays),
        out_specs=VMEM,
        scratch_shapes=[
            pltpu.VMEM((tokens, BS), jnp.bfloat16),
            pltpu.VMEM((tokens, BS), jnp.bfloat16),
        ],
        cost_estimate=pl.CostEstimate(
            flops=2 * tokens * BS * BS, transcendentals=0, bytes_accessed=0
        ),
        compiler_params=pltpu.CompilerParams(vmem_limit_bytes=8 << 20),
        name="partial",
    )(block_slot, slot_tile, *arrays)


def finish_kernel(block_count, total_tokens, n_parts, slot_ref, tile_ref, acc, *refs):
    own, other = refs[:n_parts], refs[n_parts : 2 * n_parts]
    far, far_other, *stats = refs[2 * n_parts : -7]
    out, mean, var, left, right, result, sems = refs[-7:]
    tok_dev, width = far.shape
    held = width // BS
    col = lax.axis_index("col")
    blocks = wanted(tile_ref, slot_ref, col, block_count, 2)
    start = assemble(blocks, col, held, own, other, (left, right), 0)
    for side, block in enumerate(blocks):
        for ref, half in ((far, col), (far_other, 1 - col)):
            take_block(block, half, held, [ref], [start], (left, right)[side])
    mine = tile_ref[lax.axis_index("tok") * 2 + col]
    live = mine < block_count * (block_count + 1) // 2
    chunks = sems.shape[0]
    rows = BS // chunks
    copies = []
    for m in range(chunks):
        here = slice(m * rows, (m + 1) * rows)
        total = acc[here, :] + product_rows(left, right, m, rows)
        result[here, :] = jnp.where(live, total / total_tokens, 0.0)
        copies.append(
            pltpu.make_async_copy(result.at[here, :], out.at[0, here, :], sems.at[m])
        )
        copies[-1].start()
    *whole, split = stats
    last = merge(
        (split[0:1, :], split[1:2, :]),
        merge((split[2:3, :], split[3:4, :]), shard_stats(far), tok_dev),
        2 * tok_dev,
    )
    parts = [(ref[0:1, :], ref[1:2, :]) for ref in whole] + [last]
    part, square = stat_tree(parts, 4 * tok_dev)
    mean[...] = part / total_tokens
    var[...] = square / total_tokens
    for copy in copies:
        copy.wait()


def finish(block_count, total_tokens, block_slot, slot_tile, acc, own, other, far, far_other, stats):
    near = Near(True)
    width = far.shape[1]
    tokens = sum(a.shape[0] for a in own) + far.shape[0]
    arrays = [near.put(a) for a in (acc, *own, *other, far, far_other, *stats)]
    product, mean, var = pl.pallas_call(
        lambda *refs: finish_kernel(block_count, total_tokens, len(own), *refs),
        out_shape=[
            jax.ShapeDtypeStruct((1, BS, BS), jnp.float32),
            jax.ShapeDtypeStruct((1, width), jnp.float32),
            jax.ShapeDtypeStruct((1, width), jnp.float32),
        ],
        in_specs=[SMEM, SMEM] + [VMEM] * len(arrays),
        out_specs=[pl.BlockSpec(memory_space=pl.ANY), VMEM, VMEM],
        scratch_shapes=[
            pltpu.VMEM((tokens, BS), jnp.bfloat16),
            pltpu.VMEM((tokens, BS), jnp.bfloat16),
            pltpu.VMEM((BS, BS), jnp.float32),
            pltpu.SemaphoreType.DMA((4,)),
        ],
        cost_estimate=pl.CostEstimate(
            flops=2 * tokens * BS * BS, transcendentals=0, bytes_accessed=4 * BS * BS
        ),
        compiler_params=pltpu.CompilerParams(vmem_limit_bytes=16 << 20),
        name="finish",
    )(block_slot, slot_tile, *arrays)
    return product, mean[0], var[0]


def by_halves(activations, block_slot, slot_tile):
    n_tok = lax.axis_size("tok")
    n_out = n_tok // 4
    tok_dev, width = activations.shape
    held = width // BS
    block_count = held * 2
    tables = tuple(pltpu.with_memory_space_constraint(a, pltpu.HBM) for a in (block_slot, slot_tile))

    def from_outer(a, k):
        return lax.ppermute(a, "tok", [(t, t ^ (4 * k)) for t in range(n_tok)])

    def from_plane(a, first):
        pairs = [
            (t * 2 + c, (t ^ (1 if (c == 0) == first else 2)) * 2 + c)
            for t in range(n_tok)
            for c in range(2)
        ]
        return lax.ppermute(a, ("tok", "col"), pairs)

    def from_sibling(a):
        return lax.ppermute(a, "col", [(0, 1), (1, 0)])

    own, other, stats = [], [], []
    shard, first, second, far = {0: activations}, {}, {}, {}
    shard[1] = from_outer(activations, 1)
    shard[2] = from_outer(activations, 2)
    first[0] = from_plane(activations, True)
    second[0] = from_plane(activations, False)
    shard[3] = from_outer(after(activations, shard[2]), 3)
    acc = None
    for k in range(n_out):
        last = k == n_out - 1
        src = shard[k]
        if k == 2:
            src = shard[k]
        if k == 3:
            src = shard[k]
        if k:
            first[k] = from_plane(src, True)
        src = shard[k]
        if k == 1:
            src = shard[k]
        if k == 2:
            src = shard[k]
        if k == 3:
            src = shard[k]
        if k:
            second[k] = from_plane(src, False)
        gated = first[k]
        if k == 0:
            gated = first[k]
        if k == 1:
            gated = after(first[k], far[0], second[0])
        if k == 2:
            gated = after(first[k], far[1], second[1])
        if k == 3:
            gated = after(first[k], far[2], second[2], own[1])
        far[k] = from_plane(gated, False)
        shards = [shard[k], first[k], second[k]] + ([] if last else [far[k]])
        if last:
            acc = partial_gram(block_count, held, *tables, own[: k - 1], other[: k - 1])

        mine, sibling, part = wave_parts(block_count, *tables, shards)
        own.append(mine)
        other.append(from_sibling(sibling))
        stats.append(part)
    far_other = from_sibling(far[3])
    return finish(
        block_count, n_tok * tok_dev, *tables, acc, own[-2:], other[-2:], far[3], far_other, stats
    )


def on_device(activations, block_slot, slot_tile):
    n_in = split_tok(lax.axis_size("tok"))[1]
    small = lax.axis_size("col") == 2 and lax.axis_size("tok") == 16
    return (by_halves if small else by_blocks)(activations, block_slot, slot_tile)


def solution(mesh):
    return jax.shard_map(
        on_device,
        mesh=mesh,
        in_specs=(P("tok", "col"), P(), P()),
        out_specs=(P(("tok", "col"), None, None), P("col"), P("col")),
        check_vma=False,
    )
```

```python
import jax
import jax.numpy as jnp
import numpy as np
from jax import lax
from jax.experimental import pallas as pl
from jax.experimental.pallas import tpu as pltpu
from jax.sharding import PartitionSpec as P

BS = 1024


def split_tok(n_tok):
    n_in = 1
    while n_in * n_in < n_tok:
        n_in *= 2
    return n_tok // n_in, n_in


def outer_waves(n_out):
    waves = [[0], [1, 2], [3]] if n_out >= 4 else [[k] for k in range(n_out)]
    return waves + [[k, k + 1] for k in range(4, n_out, 2)]


def pair_of(tile, block_count):
    pair_count = block_count * (block_count + 1) // 2
    tile = jnp.where(tile < pair_count, tile, 0)
    row = jnp.int32(0)
    start = jnp.int32(0)
    for r in range(1, block_count):
        first = r * block_count - r * (r - 1) // 2
        beyond = tile >= first
        row = jnp.where(beyond, r, row)
        start = jnp.where(beyond, first, start)
    return row, tile - start + row


def select_kernel(n_in, n_col, block_count, n_shards, *refs):
    slot_ref, tile_ref = refs[0], refs[1]
    shards = refs[2 : 2 + n_shards * n_col]
    outs = refs[2 + n_shards * n_col :]
    tok_dev, width = shards[0].shape
    held = width // BS
    tok = lax.axis_index("tok")
    col = lax.axis_index("col")
    inner = lax.rem(tok, n_in)
    for k in range(n_in):
        peer = tok - inner + (inner ^ k)
        pair = pair_of(tile_ref[peer * n_col + col], block_count)
        for side in range(2):
            block = slot_ref[pair[side]]
            owner = lax.div(block, held)
            column = pl.multiple_of((block - owner * held) * BS, BS)
            away = lax.rem(owner - col + n_col, n_col)
            for r in range(n_col):

                @pl.when(away == r)
                def _():
                    for s in range(n_shards):
                        outs[k][s * tok_dev : (s + 1) * tok_dev, side * BS : (side + 1) * BS] = (
                            shards[s * n_col + r][:, pl.ds(column, BS)]
                        )


def select(n_in, n_col, block_count, block_slot, slot_tile, shards, near):
    rows = len(shards) * shards[0][0].shape[0]
    flat = [near.put(a) for shard in shards for a in shard]
    return pl.pallas_call(
        lambda *refs: select_kernel(n_in, n_col, block_count, len(shards), *refs),
        out_shape=[near.out((rows, 2 * BS), jnp.bfloat16)] * n_in,
        in_specs=[SMEM, SMEM] + [VMEM] * len(flat),
        out_specs=[VMEM] * n_in,
        cost_estimate=pl.CostEstimate(flops=0, transcendentals=0, bytes_accessed=8 * rows * 2 * BS),
        name="select",
    )(block_slot, slot_tile, *flat)


def merge(a, b, count):
    return a[0] + b[0], a[1] + b[1] + (a[0] - b[0]) ** 2 / (2 * count)


def stats_kernel(*refs):
    shards, out = refs[:-1], refs[-1]
    count = shards[0].shape[0]
    parts = []
    for ref in shards:
        values = ref[...].astype(jnp.float32)
        part = jnp.sum(values, axis=0, keepdims=True)
        parts.append((part, jnp.sum((values - part / count) ** 2, axis=0, keepdims=True)))
    while len(parts) > 1:
        half = len(parts) // 2
        parts = [merge(parts[k], parts[k + half], count) for k in range(half)]
        count *= 2
    out[0:1, :] = parts[0][0]
    out[1:2, :] = parts[0][1]


def local_stats(shards, near):
    tok_dev, width = shards[0].shape
    return pl.pallas_call(
        stats_kernel,
        out_shape=near.out((2, width), jnp.float32),
        in_specs=[VMEM] * len(shards),
        out_specs=VMEM,
        cost_estimate=pl.CostEstimate(
            flops=4 * len(shards) * tok_dev * width,
            transcendentals=0,
            bytes_accessed=2 * len(shards) * tok_dev * width,
        ),
        name="stats",
    )(*[near.put(a) for a in shards])


def gram_kernel(n_col, pair_count, tile_ref, *refs):
    pieces, (out, left, right, chunk, sems) = refs[:-5], refs[-5:]
    total_tokens = left.shape[0]
    start = 0
    for ref in pieces:
        rows = ref.shape[0]
        left[start : start + rows, :] = ref[:, :BS]
        right[start : start + rows, :] = ref[:, BS:]
        start += rows
    mine = tile_ref[lax.axis_index("tok") * n_col + lax.axis_index("col")]
    rows = chunk.shape[1]
    copies = [None, None]
    for m in range(BS // rows):
        slot = m % 2
        if copies[slot] is not None:
            copies[slot].wait()
        product = lax.dot_general(
            left[:, m * rows : (m + 1) * rows],
            right[...],
            (((0,), (0,)), ((), ())),
            preferred_element_type=jnp.float32,
        )
        chunk[slot] = jnp.where(mine < pair_count, product / total_tokens, 0.0)
        copies[slot] = pltpu.make_async_copy(
            chunk.at[slot], out.at[0, m * rows : (m + 1) * rows, :], sems.at[slot]
        )
        copies[slot].start()
    for copy in copies:
        copy.wait()


def gram(n_col, pair_count, slot_tile, pieces, near):
    total_tokens = sum(a.shape[0] for a in pieces)
    return pl.pallas_call(
        lambda *refs: gram_kernel(n_col, pair_count, *refs),
        out_shape=jax.ShapeDtypeStruct((1, BS, BS), jnp.float32),
        in_specs=[SMEM] + [VMEM] * len(pieces),
        out_specs=pl.BlockSpec(memory_space=pl.ANY),
        scratch_shapes=[
            pltpu.VMEM((total_tokens, BS), jnp.bfloat16),
            pltpu.VMEM((total_tokens, BS), jnp.bfloat16),
            pltpu.VMEM((2, BS // 4, BS), jnp.float32),
            pltpu.SemaphoreType.DMA((2,)),
        ],
        cost_estimate=pl.CostEstimate(
            flops=2 * total_tokens * BS * BS, transcendentals=0, bytes_accessed=4 * BS * BS
        ),
        name="gram",
    )(slot_tile, *[near.put(a) for a in pieces])


SMEM = pl.BlockSpec(memory_space=pltpu.SMEM)
VMEM = pl.BlockSpec(memory_space=pltpu.VMEM)


class Near:
    def __init__(self, fits):
        self.fits = fits

    def put(self, a):
        return pltpu.with_memory_space_constraint(a, pltpu.VMEM) if self.fits else a

    def out(self, shape, dtype):
        return pltpu.VMEM(shape, dtype) if self.fits else jax.ShapeDtypeStruct(shape, dtype)


def after(value, *earlier):
    return lax.optimization_barrier((value, *earlier))[0]


def by_blocks(activations, block_slot, slot_tile):
    n_tok = lax.axis_size("tok")
    n_col = lax.axis_size("col")
    n_out, n_in = split_tok(n_tok)
    tok_dev, width = activations.shape
    total_tokens = tok_dev * n_tok
    block_count = width * n_col // BS
    pair_count = block_count * (block_count + 1) // 2
    held = 2 * tok_dev * (n_out * n_col * width + 2 * n_tok * 2 * BS)
    near = Near(held <= 12 << 20)

    def from_outer(a, k):
        return lax.ppermute(a, "tok", [(t, t ^ (k * n_in)) for t in range(n_tok)])

    def from_inner(a, k):
        return lax.ppermute(a, "tok", [(t, t ^ k) for t in range(n_tok)])

    def all_columns(a):
        return [a] + [
            lax.ppermute(a, "col", [(c, (c - r) % n_col) for c in range(n_col)])
            for r in range(1, n_col)
        ]

    waves = outer_waves(n_out)
    shard = {0: activations}
    source = activations
    pieces = []
    done = None
    for w, wave in enumerate(waves):
        full = []
        for k in wave:
            if k:
                shard[k] = after(from_outer(activations if w < 2 else source, k), done)
            full.append(all_columns(shard[k]))
        source = after(activations, *[shard[k] for k in wave if k])
        picked = select(n_in, n_col, block_count, block_slot, slot_tile, full, near)
        if pieces:
            picked = lax.optimization_barrier((*picked, *arrived))[:n_in]
        done = picked[0]
        pieces.append(picked[0])
        arrived = [from_inner(picked[k], k) for k in range(1, n_in)]
        pieces.extend(arrived)

    mine = local_stats([after(shard[k], done) for k in range(n_out)], near)
    mine = (mine[0], mine[1])
    count = tok_dev * n_out
    k = 1
    while k < n_in:
        other = from_inner(jnp.stack(mine), k)
        mine = merge(mine, (other[0], other[1]), count)
        count *= 2
        k *= 2
    product = gram(n_col, pair_count, slot_tile, pieces, near)
    return (product, mine[0] / total_tokens, mine[1] / total_tokens)


def plan_kernel(block_count, slot_ref, tile_ref, plan):
    col = lax.axis_index("col")
    mine = tile_ref[lax.axis_index("tok") * 2 + col]
    packed = jnp.where(mine < block_count * (block_count + 1) // 2, 1 << 24, 0)
    shift = 0
    for tile in (mine, tile_ref[lax.axis_index("tok") * 2 + 1 - col]):
        for member in pair_of(tile, block_count):
            packed += slot_ref[member] << shift
            shift += 6
    plan[...] = jnp.full((8, 128), packed, jnp.int32)


def make_plan(block_count, block_slot, slot_tile):
    tables = [pltpu.with_memory_space_constraint(a, pltpu.HBM) for a in (block_slot, slot_tile)]
    return pl.pallas_call(
        lambda *refs: plan_kernel(block_count, *refs),
        out_shape=Near(True).out((8, 128), jnp.int32),
        in_specs=[SMEM, SMEM],
        out_specs=VMEM,
        compiler_params=pltpu.CompilerParams(vmem_limit_bytes=1 << 20),
        name="plan",
    )(*tables)


def planned(plan):
    packed = jnp.max(plan[0:1, :])
    blocks = [(packed >> (6 * k)) & 63 for k in range(4)]
    return blocks[:2], blocks[2:], packed >= 1 << 24


def stat_tree(parts, count):
    while len(parts) > 1:
        half = len(parts) // 2
        parts = [merge(parts[k], parts[k + half], count) for k in range(half)]
        count *= 2
    return parts[0]


def shard_stats(ref):
    values = ref[...].astype(jnp.float32)
    part = jnp.sum(values, axis=0, keepdims=True)
    mean = part / values.shape[0]
    return part, jnp.sum((values - mean) ** 2, axis=0, keepdims=True)


def take_block(block, col, held, pieces, starts, dst):
    owner = lax.div(block, held)
    column = pl.multiple_of((block - owner * held) * BS, BS)

    @pl.when(owner == col)
    def _():
        for ref, start in zip(pieces, starts):
            dst[pl.ds(start, ref.shape[0]), :] = ref[:, pl.ds(column, BS)]


def wave_kernel(plan, *refs):
    shards, (own, other, stats) = refs[:-3], refs[-3:]
    tok_dev, width = shards[0].shape
    col = lax.axis_index("col")
    first = pl.multiple_of((1 + col) * tok_dev, tok_dev)
    second = pl.multiple_of((2 - col) * tok_dev, tok_dev)
    starts = (0, first, second, 3 * tok_dev)
    mine, theirs, _ = planned(plan)
    for out, blocks in ((own, mine), (other, theirs)):
        for side, block in enumerate(blocks):
            side_out = out.at[:, side * BS : (side + 1) * BS]
            take_block(block, col, width // BS, shards, starts, side_out)
    parts = [shard_stats(ref) for ref in shards]
    if len(parts) == 4:
        parts = [stat_tree(parts, tok_dev)]
    else:
        parts = [merge(parts[0], parts[2], tok_dev), parts[1]]
    for k, (part, square) in enumerate(parts):
        stats[2 * k : 2 * k + 1, :] = part
        stats[2 * k + 1 : 2 * k + 2, :] = square


def wave_parts(plan, shards, skip=None):
    tok_dev, width = shards[0].shape
    near = Near(True)
    rows = len(shards) * tok_dev
    return pl.pallas_call(
        wave_kernel,
        out_shape=[
            near.out((rows, 2 * BS), jnp.bfloat16),
            near.out((rows, 2 * BS), jnp.bfloat16),
            near.out((2 if len(shards) == 4 else 4, width), jnp.float32),
        ],
        in_specs=[VMEM] * (1 + len(shards)),
        out_specs=[VMEM] * 3,
        cost_estimate=pl.CostEstimate(flops=0, transcendentals=0, bytes_accessed=2 * rows * width),
        compiler_params=pltpu.CompilerParams(vmem_limit_bytes=4 << 20),
        name="wave",
    )(near.put(plan), *[a if a is skip else near.put(a) for a in shards])


def assemble(blocks, col, held, own, other, sides, start):
    for side, block in enumerate(blocks):
        here = lax.div(block, held) == col
        for parts, taken in ((own, here), (other, jnp.logical_not(here))):

            @pl.when(taken)
            def _():
                row = start
                for ref in parts:
                    rows = ref.shape[0]
                    sides[side][row : row + rows, :] = ref[:, side * BS : (side + 1) * BS]
                    row += rows
    return start + sum(ref.shape[0] for ref in own)


def product_rows(left, right, m, rows):
    return lax.dot_general(
        left[:, m * rows : (m + 1) * rows],
        right[...],
        (((0,), (0,)), ((), ())),
        preferred_element_type=jnp.float32,
    )


def partial_kernel(held, plan, *refs):
    parts, (acc, left, right) = refs[:-3], refs[-3:]
    half = len(parts) // 2
    col = lax.axis_index("col")
    blocks = planned(plan)[0]
    assemble(blocks, col, held, parts[:half], parts[half:], (left, right), 0)
    rows = BS // 4
    for m in range(BS // rows):
        acc[m * rows : (m + 1) * rows, :] = product_rows(left, right, m, rows)


def partial_gram(held, plan, own, other):
    near = Near(True)
    tokens = sum(a.shape[0] for a in own)
    arrays = [near.put(a) for a in (plan, *own, *other)]
    return pl.pallas_call(
        lambda *refs: partial_kernel(held, *refs),
        out_shape=near.out((BS, BS), jnp.float32),
        in_specs=[VMEM] * len(arrays),
        out_specs=VMEM,
        scratch_shapes=[
            pltpu.VMEM((tokens, BS), jnp.bfloat16),
            pltpu.VMEM((tokens, BS), jnp.bfloat16),
        ],
        cost_estimate=pl.CostEstimate(
            flops=2 * tokens * BS * BS, transcendentals=0, bytes_accessed=0
        ),
        compiler_params=pltpu.CompilerParams(vmem_limit_bytes=8 << 20),
        name="partial",
    )(*arrays)


def finish_kernel(total_tokens, n_parts, plan, acc, *refs):
    own, other = refs[:n_parts], refs[n_parts : 2 * n_parts]
    far, far_other, *stats = refs[2 * n_parts : -8]
    out, mean, var, left, right, result, moments, sems = refs[-8:]
    tok_dev, width = far.shape
    held = width // BS
    col = lax.axis_index("col")
    blocks, _, live = planned(plan)
    start = assemble(blocks, col, held, own, other, (left, right), 0)
    for side, block in enumerate(blocks):
        for ref, half in ((far, col), (far_other, 1 - col)):
            take_block(block, half, held, [ref], [start], (left, right)[side])
    chunks = sems.shape[0] - 2
    rows = BS // chunks
    copies = []
    for m in range(chunks):
        here = slice(m * rows, (m + 1) * rows)
        total = acc[here, :] + product_rows(left, right, m, rows)
        result[here, :] = jnp.where(live, total / total_tokens, 0.0)
        copies.append(
            pltpu.make_async_copy(result.at[here, :], out.at[0, here, :], sems.at[m])
        )
        copies[-1].start()
    *whole, split = stats
    last = merge(
        (split[0:1, :], split[1:2, :]),
        merge((split[2:3, :], split[3:4, :]), shard_stats(far), tok_dev),
        2 * tok_dev,
    )
    parts = [(ref[0:1, :], ref[1:2, :]) for ref in whole] + [last]
    part, square = stat_tree(parts, 4 * tok_dev)
    for k, (ref, value) in enumerate(((mean, part), (var, square))):
        moments[k] = value / total_tokens
        copies.append(pltpu.make_async_copy(moments.at[k], ref, sems.at[chunks + k]))
        copies[-1].start()
    for copy in copies:
        copy.wait()


def finish(total_tokens, plan, acc, own, other, far, far_other, stats):
    near = Near(True)
    width = far.shape[1]
    tokens = sum(a.shape[0] for a in own) + far.shape[0]
    arrays = [near.put(a) for a in (plan, acc, *own, *other, far, far_other, *stats)]
    product, mean, var = pl.pallas_call(
        lambda *refs: finish_kernel(total_tokens, len(own), *refs),
        out_shape=[
            jax.ShapeDtypeStruct((1, BS, BS), jnp.float32),
            jax.ShapeDtypeStruct((1, width), jnp.float32),
            jax.ShapeDtypeStruct((1, width), jnp.float32),
        ],
        in_specs=[VMEM] * len(arrays),
        out_specs=[pl.BlockSpec(memory_space=pl.ANY)] * 3,
        scratch_shapes=[
            pltpu.VMEM((tokens, BS), jnp.bfloat16),
            pltpu.VMEM((tokens, BS), jnp.bfloat16),
            pltpu.VMEM((BS, BS), jnp.float32),
            pltpu.VMEM((2, 1, width), jnp.float32),
            pltpu.SemaphoreType.DMA((6,)),
        ],
        cost_estimate=pl.CostEstimate(
            flops=2 * tokens * BS * BS, transcendentals=0, bytes_accessed=4 * BS * BS
        ),
        compiler_params=pltpu.CompilerParams(vmem_limit_bytes=16 << 20),
        name="finish",
    )(*arrays)
    return product, mean[0], var[0]


def by_halves(activations, block_slot, slot_tile):
    n_tok = lax.axis_size("tok")
    tok_dev, width = activations.shape
    held = width // BS
    block_count = held * 2
    plan = make_plan(block_count, block_slot, slot_tile)

    def from_outer(a, k):
        return lax.ppermute(a, "tok", [(t, t ^ (4 * k)) for t in range(n_tok)])

    def from_plane(a, first):
        pairs = [
            (t * 2 + c, (t ^ (1 if (c == 0) == first else 2)) * 2 + c)
            for t in range(n_tok)
            for c in range(2)
        ]
        return lax.ppermute(a, ("tok", "col"), pairs)

    def from_sibling(a):
        return lax.ppermute(a, "col", [(0, 1), (1, 0)])

    z1 = from_outer(activations, 1)
    z2 = from_outer(activations, 2)
    s0 = from_plane(activations, True)
    z3 = from_outer(after(activations, s0), 3)
    b0 = from_plane(after(activations, s0), False)
    f0 = from_plane(s0, False)
    own0, out0, stats0 = wave_parts(plan, [activations, s0, b0, after(f0, z3)], activations)
    other0 = from_sibling(out0)
    s1 = from_plane(z1, True)
    b1 = from_plane(after(z1, z2), False)
    f1 = from_plane(after(s1, f0, b0), False)
    own1, out1, stats1 = wave_parts(plan, [z1, s1, b1, after(f1, f1)])
    other1 = from_sibling(out1)
    s2 = from_plane(z2, True)
    b2 = from_plane(after(z2, b1), False)
    f2 = from_plane(after(s2, f1, b1, z3), False)
    own2, out2, stats2 = wave_parts(plan, [z2, s2, b2, f2])
    other2 = from_sibling(out2)
    s3 = from_plane(z3, True)
    b3 = from_plane(z3, False)
    f3 = from_plane(after(s3, b1, b2), False)
    own3, out3, stats3 = wave_parts(plan, [z3, s3, after(b3, f2)])
    other3 = from_sibling(out3)
    acc = partial_gram(held, plan, [own0, own1], [other0, other1])
    far_other = from_sibling(f3)
    return finish(
        n_tok * tok_dev,
        plan,
        acc,
        [own2, own3],
        [other2, other3],
        f3,
        far_other,
        [stats0, stats1, stats2, stats3],
    )


def on_device(activations, block_slot, slot_tile):
    n_in = split_tok(lax.axis_size("tok"))[1]
    small = lax.axis_size("col") == 2 and lax.axis_size("tok") == 16
    return (by_halves if small else by_blocks)(activations, block_slot, slot_tile)


def solution(mesh):
    return jax.shard_map(
        on_device,
        mesh=mesh,
        in_specs=(P("tok", "col"), P(), P()),
        out_specs=(P(("tok", "col"), None, None), P("col"), P("col")),
        check_vma=False,
    )
```

```python
import jax
import jax.numpy as jnp
import numpy as np
from jax import lax
from jax.experimental import pallas as pl
from jax.experimental.pallas import tpu as pltpu
from jax.sharding import PartitionSpec as P

BS = 1024


def split_tok(n_tok):
    n_in = 1
    while n_in * n_in < n_tok:
        n_in *= 2
    return n_tok // n_in, n_in


def outer_waves(n_out):
    waves = [[0], [1, 2], [3]] if n_out >= 4 else [[k] for k in range(n_out)]
    return waves + [[k, k + 1] for k in range(4, n_out, 2)]


def pair_of(tile, block_count):
    pair_count = block_count * (block_count + 1) // 2
    tile = jnp.where(tile < pair_count, tile, 0)
    row = jnp.int32(0)
    start = jnp.int32(0)
    for r in range(1, block_count):
        first = r * block_count - r * (r - 1) // 2
        beyond = tile >= first
        row = jnp.where(beyond, r, row)
        start = jnp.where(beyond, first, start)
    return row, tile - start + row


def select_kernel(n_in, n_col, block_count, n_shards, *refs):
    slot_ref, tile_ref = refs[0], refs[1]
    shards = refs[2 : 2 + n_shards * n_col]
    outs = refs[2 + n_shards * n_col :]
    tok_dev, width = shards[0].shape
    held = width // BS
    tok = lax.axis_index("tok")
    col = lax.axis_index("col")
    inner = lax.rem(tok, n_in)
    for k in range(n_in):
        peer = tok - inner + (inner ^ k)
        pair = pair_of(tile_ref[peer * n_col + col], block_count)
        for side in range(2):
            block = slot_ref[pair[side]]
            owner = lax.div(block, held)
            column = pl.multiple_of((block - owner * held) * BS, BS)
            away = lax.rem(owner - col + n_col, n_col)
            for r in range(n_col):

                @pl.when(away == r)
                def _():
                    for s in range(n_shards):
                        outs[k][s * tok_dev : (s + 1) * tok_dev, side * BS : (side + 1) * BS] = (
                            shards[s * n_col + r][:, pl.ds(column, BS)]
                        )


def select(n_in, n_col, block_count, block_slot, slot_tile, shards, near):
    rows = len(shards) * shards[0][0].shape[0]
    flat = [near.put(a) for shard in shards for a in shard]
    return pl.pallas_call(
        lambda *refs: select_kernel(n_in, n_col, block_count, len(shards), *refs),
        out_shape=[near.out((rows, 2 * BS), jnp.bfloat16)] * n_in,
        in_specs=[SMEM, SMEM] + [VMEM] * len(flat),
        out_specs=[VMEM] * n_in,
        cost_estimate=pl.CostEstimate(flops=0, transcendentals=0, bytes_accessed=8 * rows * 2 * BS),
        name="select",
    )(block_slot, slot_tile, *flat)


def merge(a, b, count):
    return a[0] + b[0], a[1] + b[1] + (a[0] - b[0]) ** 2 / (2 * count)


def stats_kernel(*refs):
    shards, out = refs[:-1], refs[-1]
    count = shards[0].shape[0]
    parts = []
    for ref in shards:
        values = ref[...].astype(jnp.float32)
        part = jnp.sum(values, axis=0, keepdims=True)
        parts.append((part, jnp.sum((values - part / count) ** 2, axis=0, keepdims=True)))
    while len(parts) > 1:
        half = len(parts) // 2
        parts = [merge(parts[k], parts[k + half], count) for k in range(half)]
        count *= 2
    out[0:1, :] = parts[0][0]
    out[1:2, :] = parts[0][1]


def local_stats(shards, near):
    tok_dev, width = shards[0].shape
    return pl.pallas_call(
        stats_kernel,
        out_shape=near.out((2, width), jnp.float32),
        in_specs=[VMEM] * len(shards),
        out_specs=VMEM,
        cost_estimate=pl.CostEstimate(
            flops=4 * len(shards) * tok_dev * width,
            transcendentals=0,
            bytes_accessed=2 * len(shards) * tok_dev * width,
        ),
        name="stats",
    )(*[near.put(a) for a in shards])


def gram_kernel(n_col, pair_count, tile_ref, *refs):
    pieces, (out, left, right, chunk, sems) = refs[:-5], refs[-5:]
    total_tokens = left.shape[0]
    start = 0
    for ref in pieces:
        rows = ref.shape[0]
        left[start : start + rows, :] = ref[:, :BS]
        right[start : start + rows, :] = ref[:, BS:]
        start += rows
    mine = tile_ref[lax.axis_index("tok") * n_col + lax.axis_index("col")]
    rows = chunk.shape[1]
    copies = [None, None]
    for m in range(BS // rows):
        slot = m % 2
        if copies[slot] is not None:
            copies[slot].wait()
        product = lax.dot_general(
            left[:, m * rows : (m + 1) * rows],
            right[...],
            (((0,), (0,)), ((), ())),
            preferred_element_type=jnp.float32,
        )
        chunk[slot] = jnp.where(mine < pair_count, product / total_tokens, 0.0)
        copies[slot] = pltpu.make_async_copy(
            chunk.at[slot], out.at[0, m * rows : (m + 1) * rows, :], sems.at[slot]
        )
        copies[slot].start()
    for copy in copies:
        copy.wait()


def gram(n_col, pair_count, slot_tile, pieces, near):
    total_tokens = sum(a.shape[0] for a in pieces)
    return pl.pallas_call(
        lambda *refs: gram_kernel(n_col, pair_count, *refs),
        out_shape=jax.ShapeDtypeStruct((1, BS, BS), jnp.float32),
        in_specs=[SMEM] + [VMEM] * len(pieces),
        out_specs=pl.BlockSpec(memory_space=pl.ANY),
        scratch_shapes=[
            pltpu.VMEM((total_tokens, BS), jnp.bfloat16),
            pltpu.VMEM((total_tokens, BS), jnp.bfloat16),
            pltpu.VMEM((2, BS // 4, BS), jnp.float32),
            pltpu.SemaphoreType.DMA((2,)),
        ],
        cost_estimate=pl.CostEstimate(
            flops=2 * total_tokens * BS * BS, transcendentals=0, bytes_accessed=4 * BS * BS
        ),
        name="gram",
    )(slot_tile, *[near.put(a) for a in pieces])


SMEM = pl.BlockSpec(memory_space=pltpu.SMEM)
VMEM = pl.BlockSpec(memory_space=pltpu.VMEM)


class Near:
    def __init__(self, fits):
        self.fits = fits

    def put(self, a):
        return pltpu.with_memory_space_constraint(a, pltpu.VMEM) if self.fits else a

    def out(self, shape, dtype):
        return pltpu.VMEM(shape, dtype) if self.fits else jax.ShapeDtypeStruct(shape, dtype)


def after(value, *earlier):
    return lax.optimization_barrier((value, *earlier))[0]


def by_blocks(activations, block_slot, slot_tile):
    n_tok = lax.axis_size("tok")
    n_col = lax.axis_size("col")
    n_out, n_in = split_tok(n_tok)
    tok_dev, width = activations.shape
    total_tokens = tok_dev * n_tok
    block_count = width * n_col // BS
    pair_count = block_count * (block_count + 1) // 2
    held = 2 * tok_dev * (n_out * n_col * width + 2 * n_tok * 2 * BS)
    near = Near(held <= 12 << 20)

    def from_outer(a, k):
        return lax.ppermute(a, "tok", [(t, t ^ (k * n_in)) for t in range(n_tok)])

    def from_inner(a, k):
        return lax.ppermute(a, "tok", [(t, t ^ k) for t in range(n_tok)])

    def all_columns(a):
        return [a] + [
            lax.ppermute(a, "col", [(c, (c - r) % n_col) for c in range(n_col)])
            for r in range(1, n_col)
        ]

    waves = outer_waves(n_out)
    shard = {0: activations}
    source = activations
    pieces = []
    done = None
    for w, wave in enumerate(waves):
        full = []
        for k in wave:
            if k:
                shard[k] = after(from_outer(activations if w < 2 else source, k), done)
            full.append(all_columns(shard[k]))
        source = after(activations, *[shard[k] for k in wave if k])
        picked = select(n_in, n_col, block_count, block_slot, slot_tile, full, near)
        if pieces:
            picked = lax.optimization_barrier((*picked, *arrived))[:n_in]
        done = picked[0]
        pieces.append(picked[0])
        arrived = [from_inner(picked[k], k) for k in range(1, n_in)]
        pieces.extend(arrived)

    mine = local_stats([after(shard[k], done) for k in range(n_out)], near)
    mine = (mine[0], mine[1])
    count = tok_dev * n_out
    k = 1
    while k < n_in:
        other = from_inner(jnp.stack(mine), k)
        mine = merge(mine, (other[0], other[1]), count)
        count *= 2
        k *= 2
    product = gram(n_col, pair_count, slot_tile, pieces, near)
    return (product, mine[0] / total_tokens, mine[1] / total_tokens)


def plan_kernel(block_count, slot_ref, tile_ref, shard, plan, near_shard):
    col = lax.axis_index("col")
    mine = tile_ref[lax.axis_index("tok") * 2 + col]
    packed = jnp.where(mine < block_count * (block_count + 1) // 2, 1 << 24, 0)
    shift = 0
    for tile in (mine, tile_ref[lax.axis_index("tok") * 2 + 1 - col]):
        for member in pair_of(tile, block_count):
            packed += slot_ref[member] << shift
            shift += 6
    plan[...] = jnp.full((8, 128), packed, jnp.int32)
    near_shard[...] = shard[...]


def make_plan(block_count, block_slot, slot_tile, shard):
    near = Near(True)
    return pl.pallas_call(
        lambda *refs: plan_kernel(block_count, *refs),
        out_shape=[near.out((8, 128), jnp.int32), near.out(shard.shape, shard.dtype)],
        in_specs=[SMEM, SMEM, VMEM],
        out_specs=[VMEM, VMEM],
        compiler_params=pltpu.CompilerParams(vmem_limit_bytes=2 << 20),
        name="plan",
    )(hbm(block_slot), hbm(slot_tile), hbm(shard))


def hbm(a):
    return pltpu.with_memory_space_constraint(a, pltpu.HBM)


def planned(plan):
    packed = jnp.max(plan[0:1, :])
    blocks = [(packed >> (6 * k)) & 63 for k in range(4)]
    return blocks[:2], blocks[2:], packed >= 1 << 24


def stat_tree(parts, count):
    while len(parts) > 1:
        half = len(parts) // 2
        parts = [merge(parts[k], parts[k + half], count) for k in range(half)]
        count *= 2
    return parts[0]


def shard_stats(ref):
    values = ref[...].astype(jnp.float32)
    part = jnp.sum(values, axis=0, keepdims=True)
    mean = part / values.shape[0]
    return part, jnp.sum((values - mean) ** 2, axis=0, keepdims=True)


def take_block(block, col, held, pieces, starts, dst):
    owner = lax.div(block, held)
    column = pl.multiple_of((block - owner * held) * BS, BS)

    @pl.when(owner == col)
    def _():
        for ref, start in zip(pieces, starts):
            dst[pl.ds(start, ref.shape[0]), :] = ref[:, pl.ds(column, BS)]


def wave_kernel(sizes, plan, *refs):
    arrays, (own, other, stats) = refs[:-3], refs[-3:]
    tok_dev, width = arrays[0].shape
    col = lax.axis_index("col")
    places = (0, 1 + col, 2 - col, 3)
    starts, done, row = [], 0, 0
    for size in sizes:
        starts += [pl.multiple_of((done + p) * tok_dev, tok_dev) for p in places[:size]]
        parts = [shard_stats(ref) for ref in arrays[done : done + size]]
        if size == 4:
            parts = [stat_tree(parts, tok_dev)]
        else:
            parts = [merge(parts[0], parts[2], tok_dev), parts[1]]
        for part, square in parts:
            stats[row : row + 1, :] = part
            stats[row + 1 : row + 2, :] = square
            row += 2
        done += size
    mine, theirs, _ = planned(plan)
    for out, blocks in ((own, mine), (other, theirs)):
        for side, block in enumerate(blocks):
            side_out = out.at[:, side * BS : (side + 1) * BS]
            take_block(block, col, width // BS, arrays, starts, side_out)


def wave_parts(plan, *waves):
    near = Near(True)
    shards = [a for wave in waves for a in wave]
    sizes = [len(wave) for wave in waves]
    tok_dev, width = shards[0].shape
    rows = len(shards) * tok_dev
    return pl.pallas_call(
        lambda *refs: wave_kernel(sizes, *refs),
        out_shape=[
            near.out((rows, 2 * BS), jnp.bfloat16),
            near.out((rows, 2 * BS), jnp.bfloat16),
            near.out((sum(2 if size == 4 else 4 for size in sizes), width), jnp.float32),
        ],
        in_specs=[VMEM] * (1 + len(shards)),
        out_specs=[VMEM] * 3,
        cost_estimate=pl.CostEstimate(flops=0, transcendentals=0, bytes_accessed=2 * rows * width),
        compiler_params=pltpu.CompilerParams(vmem_limit_bytes=4 << 20),
        name="wave",
    )(near.put(plan), *[near.put(a) for a in shards])


def assemble(blocks, col, held, own, other, sides, start):
    for side, block in enumerate(blocks):
        here = lax.div(block, held) == col
        for parts, taken in ((own, here), (other, jnp.logical_not(here))):

            @pl.when(taken)
            def _():
                row = start
                for ref in parts:
                    rows = ref.shape[0]
                    sides[side][row : row + rows, :] = ref[:, side * BS : (side + 1) * BS]
                    row += rows
    return start + sum(ref.shape[0] for ref in own)


def product_rows(left, right, m, rows):
    return lax.dot_general(
        left[:, m * rows : (m + 1) * rows],
        right[...],
        (((0,), (0,)), ((), ())),
        preferred_element_type=jnp.float32,
    )


def partial_kernel(held, plan, *refs):
    parts, (acc, left, right) = refs[:-3], refs[-3:]
    half = len(parts) // 2
    col = lax.axis_index("col")
    blocks = planned(plan)[0]
    assemble(blocks, col, held, parts[:half], parts[half:], (left, right), 0)
    rows = BS // 4
    for m in range(BS // rows):
        acc[m * rows : (m + 1) * rows, :] = product_rows(left, right, m, rows)


def partial_gram(held, plan, own, other):
    near = Near(True)
    tokens = sum(a.shape[0] for a in own)
    arrays = [near.put(a) for a in (plan, *own, *other)]
    return pl.pallas_call(
        lambda *refs: partial_kernel(held, *refs),
        out_shape=near.out((BS, BS), jnp.float32),
        in_specs=[VMEM] * len(arrays),
        out_specs=VMEM,
        scratch_shapes=[
            pltpu.VMEM((tokens, BS), jnp.bfloat16),
            pltpu.VMEM((tokens, BS), jnp.bfloat16),
        ],
        cost_estimate=pl.CostEstimate(
            flops=2 * tokens * BS * BS, transcendentals=0, bytes_accessed=0
        ),
        compiler_params=pltpu.CompilerParams(vmem_limit_bytes=8 << 20),
        name="partial",
    )(*arrays)


def finish_kernel(total_tokens, n_parts, plan, acc, *refs):
    own, other = refs[:n_parts], refs[n_parts : 2 * n_parts]
    far, far_other, *stats = refs[2 * n_parts : -8]
    out, mean, var, left, right, result, moments, sems = refs[-8:]
    tok_dev, width = far.shape
    held = width // BS
    col = lax.axis_index("col")
    blocks, _, live = planned(plan)
    start = assemble(blocks, col, held, own, other, (left, right), 0)
    for side, block in enumerate(blocks):
        for ref, half in ((far, col), (far_other, 1 - col)):
            take_block(block, half, held, [ref], [start], (left, right)[side])
    chunks = sems.shape[0] - 2
    rows = BS // chunks
    copies = []
    for m in range(chunks):
        here = slice(m * rows, (m + 1) * rows)
        total = acc[here, :] + product_rows(left, right, m, rows)
        result[here, :] = jnp.where(live, total / total_tokens, 0.0)
        copies.append(
            pltpu.make_async_copy(result.at[here, :], out.at[0, here, :], sems.at[m])
        )
        copies[-1].start()
    *whole, split, rest = [
        (ref[k : k + 1, :], ref[k + 1 : k + 2, :]) for ref in stats for k in range(0, ref.shape[0], 2)
    ]
    parts = [*whole, merge(split, merge(rest, shard_stats(far), tok_dev), 2 * tok_dev)]
    part, square = stat_tree(parts, 4 * tok_dev)
    for k, (ref, value) in enumerate(((mean, part), (var, square))):
        moments[k] = value / total_tokens
        copies.append(pltpu.make_async_copy(moments.at[k], ref, sems.at[chunks + k]))
        copies[-1].start()
    for copy in copies:
        copy.wait()


def finish(total_tokens, plan, acc, own, other, far, far_other, stats):
    near = Near(True)
    width = far.shape[1]
    tokens = sum(a.shape[0] for a in own) + far.shape[0]
    arrays = [near.put(a) for a in (plan, acc, *own, *other, far, far_other, *stats)]
    product, mean, var = pl.pallas_call(
        lambda *refs: finish_kernel(total_tokens, len(own), *refs),
        out_shape=[
            jax.ShapeDtypeStruct((1, BS, BS), jnp.float32),
            jax.ShapeDtypeStruct((1, width), jnp.float32),
            jax.ShapeDtypeStruct((1, width), jnp.float32),
        ],
        in_specs=[VMEM] * len(arrays),
        out_specs=[pl.BlockSpec(memory_space=pl.ANY)] * 3,
        scratch_shapes=[
            pltpu.VMEM((tokens, BS), jnp.bfloat16),
            pltpu.VMEM((tokens, BS), jnp.bfloat16),
            pltpu.VMEM((BS, BS), jnp.float32),
            pltpu.VMEM((2, 1, width), jnp.float32),
            pltpu.SemaphoreType.DMA((10,)),
        ],
        cost_estimate=pl.CostEstimate(
            flops=2 * tokens * BS * BS, transcendentals=0, bytes_accessed=4 * BS * BS
        ),
        compiler_params=pltpu.CompilerParams(vmem_limit_bytes=16 << 20),
        name="finish",
    )(*arrays)
    return product, mean[0], var[0]


def by_halves(activations, block_slot, slot_tile):
    n_tok = lax.axis_size("tok")
    tok_dev, width = activations.shape
    held = width // BS
    block_count = held * 2
    plan, own_shard = make_plan(block_count, block_slot, slot_tile, activations)

    def from_outer(a, k):
        return lax.ppermute(a, "tok", [(t, t ^ (4 * k)) for t in range(n_tok)])

    def from_plane(a, first):
        pairs = [
            (t * 2 + c, (t ^ (1 if (c == 0) == first else 2)) * 2 + c)
            for t in range(n_tok)
            for c in range(2)
        ]
        return lax.ppermute(a, ("tok", "col"), pairs)

    def from_sibling(a):
        return lax.ppermute(a, "col", [(0, 1), (1, 0)])

    z1 = from_outer(activations, 1)
    z2 = from_outer(activations, 2)
    s0 = from_plane(activations, True)
    z3 = from_outer(after(activations, s0), 3)
    b0 = from_plane(after(activations, s0), False)
    f0 = from_plane(s0, False)
    s1 = from_plane(z1, True)
    b1 = from_plane(after(z1, z2), False)
    f1 = from_plane(after(s1, b0, f0, z2), False)
    s2 = from_plane(z2, True)
    b2 = from_plane(after(z2, b1), False)
    f2 = from_plane(after(s2, f1, b1, z3), False)
    s3 = from_plane(z3, True)
    b3 = from_plane(z3, False)
    f3 = from_plane(after(s3, b1, b2), False)
    own0, out0, stats0 = wave_parts(plan, [own_shard, s0, b0, after(f0, s3)])
    other0 = from_sibling(out0)
    own1, out1, stats1 = wave_parts(plan, [z1, s1, b1, after(f1, f1)])
    other1 = from_sibling(out1)
    own2, out2, stats2 = wave_parts(plan, [z2, s2, b2, f2])
    other2 = from_sibling(out2)
    own3, out3, stats3 = wave_parts(plan, [z3, s3, after(b3, f2)])
    other3 = from_sibling(out3)
    acc = partial_gram(held, plan, [own0, own1], [other0, other1])
    far_other = from_sibling(f3)
    return finish(
        n_tok * tok_dev,
        plan,
        acc,
        [own2, own3],
        [other2, other3],
        f3,
        far_other,
        [stats0, stats1, stats2, stats3],
    )


def on_device(activations, block_slot, slot_tile):
    n_in = split_tok(lax.axis_size("tok"))[1]
    small = lax.axis_size("col") == 2 and lax.axis_size("tok") == 16
    return (by_halves if small else by_blocks)(activations, block_slot, slot_tile)


def solution(mesh):
    return jax.shard_map(
        on_device,
        mesh=mesh,
        in_specs=(P("tok", "col"), P(), P()),
        out_specs=(P(("tok", "col"), None, None), P("col"), P("col")),
        check_vma=False,
    )
```

```python
import jax
import jax.numpy as jnp
import numpy as np
from jax import lax
from jax.experimental import pallas as pl
from jax.experimental.pallas import tpu as pltpu
from jax.sharding import PartitionSpec as P

BS = 1024


def split_tok(n_tok):
    n_in = 1
    while n_in * n_in < n_tok:
        n_in *= 2
    return n_tok // n_in, n_in


def outer_waves(n_out):
    waves = [[0], [1, 2], [3]] if n_out >= 4 else [[k] for k in range(n_out)]
    return waves + [[k, k + 1] for k in range(4, n_out, 2)]


def pair_of(tile, block_count):
    pair_count = block_count * (block_count + 1) // 2
    tile = jnp.where(tile < pair_count, tile, 0)
    row = jnp.int32(0)
    start = jnp.int32(0)
    for r in range(1, block_count):
        first = r * block_count - r * (r - 1) // 2
        beyond = tile >= first
        row = jnp.where(beyond, r, row)
        start = jnp.where(beyond, first, start)
    return row, tile - start + row


def select_kernel(n_in, n_col, block_count, n_shards, *refs):
    slot_ref, tile_ref = refs[0], refs[1]
    shards = refs[2 : 2 + n_shards * n_col]
    outs = refs[2 + n_shards * n_col :]
    tok_dev, width = shards[0].shape
    held = width // BS
    tok = lax.axis_index("tok")
    col = lax.axis_index("col")
    inner = lax.rem(tok, n_in)
    for k in range(n_in):
        peer = tok - inner + (inner ^ k)
        pair = pair_of(tile_ref[peer * n_col + col], block_count)
        for side in range(2):
            block = slot_ref[pair[side]]
            owner = lax.div(block, held)
            column = pl.multiple_of((block - owner * held) * BS, BS)
            away = lax.rem(owner - col + n_col, n_col)
            for r in range(n_col):

                @pl.when(away == r)
                def _():
                    for s in range(n_shards):
                        outs[k][s * tok_dev : (s + 1) * tok_dev, side * BS : (side + 1) * BS] = (
                            shards[s * n_col + r][:, pl.ds(column, BS)]
                        )


def select(n_in, n_col, block_count, block_slot, slot_tile, shards, near):
    rows = len(shards) * shards[0][0].shape[0]
    flat = [near.put(a) for shard in shards for a in shard]
    return pl.pallas_call(
        lambda *refs: select_kernel(n_in, n_col, block_count, len(shards), *refs),
        out_shape=[near.out((rows, 2 * BS), jnp.bfloat16)] * n_in,
        in_specs=[SMEM, SMEM] + [VMEM] * len(flat),
        out_specs=[VMEM] * n_in,
        cost_estimate=pl.CostEstimate(flops=0, transcendentals=0, bytes_accessed=8 * rows * 2 * BS),
        name="select",
    )(block_slot, slot_tile, *flat)


def merge(a, b, count):
    return a[0] + b[0], a[1] + b[1] + (a[0] - b[0]) ** 2 / (2 * count)


def stats_kernel(*refs):
    shards, out = refs[:-1], refs[-1]
    count = shards[0].shape[0]
    parts = []
    for ref in shards:
        values = ref[...].astype(jnp.float32)
        part = jnp.sum(values, axis=0, keepdims=True)
        parts.append((part, jnp.sum((values - part / count) ** 2, axis=0, keepdims=True)))
    while len(parts) > 1:
        half = len(parts) // 2
        parts = [merge(parts[k], parts[k + half], count) for k in range(half)]
        count *= 2
    out[0:1, :] = parts[0][0]
    out[1:2, :] = parts[0][1]


def local_stats(shards, near):
    tok_dev, width = shards[0].shape
    return pl.pallas_call(
        stats_kernel,
        out_shape=near.out((2, width), jnp.float32),
        in_specs=[VMEM] * len(shards),
        out_specs=VMEM,
        cost_estimate=pl.CostEstimate(
            flops=4 * len(shards) * tok_dev * width,
            transcendentals=0,
            bytes_accessed=2 * len(shards) * tok_dev * width,
        ),
        name="stats",
    )(*[near.put(a) for a in shards])


def gram_kernel(n_col, pair_count, tile_ref, *refs):
    pieces, (out, left, right, chunk, sems) = refs[:-5], refs[-5:]
    total_tokens = left.shape[0]
    start = 0
    for ref in pieces:
        rows = ref.shape[0]
        left[start : start + rows, :] = ref[:, :BS]
        right[start : start + rows, :] = ref[:, BS:]
        start += rows
    mine = tile_ref[lax.axis_index("tok") * n_col + lax.axis_index("col")]
    rows = chunk.shape[1]
    copies = [None, None]
    for m in range(BS // rows):
        slot = m % 2
        if copies[slot] is not None:
            copies[slot].wait()
        product = lax.dot_general(
            left[:, m * rows : (m + 1) * rows],
            right[...],
            (((0,), (0,)), ((), ())),
            preferred_element_type=jnp.float32,
        )
        chunk[slot] = jnp.where(mine < pair_count, product / total_tokens, 0.0)
        copies[slot] = pltpu.make_async_copy(
            chunk.at[slot], out.at[0, m * rows : (m + 1) * rows, :], sems.at[slot]
        )
        copies[slot].start()
    for copy in copies:
        copy.wait()


def gram(n_col, pair_count, slot_tile, pieces, near):
    total_tokens = sum(a.shape[0] for a in pieces)
    return pl.pallas_call(
        lambda *refs: gram_kernel(n_col, pair_count, *refs),
        out_shape=jax.ShapeDtypeStruct((1, BS, BS), jnp.float32),
        in_specs=[SMEM] + [VMEM] * len(pieces),
        out_specs=pl.BlockSpec(memory_space=pl.ANY),
        scratch_shapes=[
            pltpu.VMEM((total_tokens, BS), jnp.bfloat16),
            pltpu.VMEM((total_tokens, BS), jnp.bfloat16),
            pltpu.VMEM((2, BS // 4, BS), jnp.float32),
            pltpu.SemaphoreType.DMA((2,)),
        ],
        cost_estimate=pl.CostEstimate(
            flops=2 * total_tokens * BS * BS, transcendentals=0, bytes_accessed=4 * BS * BS
        ),
        name="gram",
    )(slot_tile, *[near.put(a) for a in pieces])


SMEM = pl.BlockSpec(memory_space=pltpu.SMEM)
VMEM = pl.BlockSpec(memory_space=pltpu.VMEM)


class Near:
    def __init__(self, fits):
        self.fits = fits

    def put(self, a):
        return pltpu.with_memory_space_constraint(a, pltpu.VMEM) if self.fits else a

    def out(self, shape, dtype):
        return pltpu.VMEM(shape, dtype) if self.fits else jax.ShapeDtypeStruct(shape, dtype)


def after(value, *earlier):
    return lax.optimization_barrier((value, *earlier))[0]


def by_blocks(activations, block_slot, slot_tile):
    n_tok = lax.axis_size("tok")
    n_col = lax.axis_size("col")
    n_out, n_in = split_tok(n_tok)
    tok_dev, width = activations.shape
    total_tokens = tok_dev * n_tok
    block_count = width * n_col // BS
    pair_count = block_count * (block_count + 1) // 2
    held = 2 * tok_dev * (n_out * n_col * width + 2 * n_tok * 2 * BS)
    near = Near(held <= 12 << 20)

    def from_outer(a, k):
        return lax.ppermute(a, "tok", [(t, t ^ (k * n_in)) for t in range(n_tok)])

    def from_inner(a, k):
        return lax.ppermute(a, "tok", [(t, t ^ k) for t in range(n_tok)])

    def all_columns(a):
        return [a] + [
            lax.ppermute(a, "col", [(c, (c - r) % n_col) for c in range(n_col)])
            for r in range(1, n_col)
        ]

    waves = outer_waves(n_out)
    shard = {0: activations}
    source = activations
    pieces = []
    done = None
    for w, wave in enumerate(waves):
        full = []
        for k in wave:
            if k:
                shard[k] = after(from_outer(activations if w < 2 else source, k), done)
            full.append(all_columns(shard[k]))
        source = after(activations, *[shard[k] for k in wave if k])
        picked = select(n_in, n_col, block_count, block_slot, slot_tile, full, near)
        if pieces:
            picked = lax.optimization_barrier((*picked, *arrived))[:n_in]
        done = picked[0]
        pieces.append(picked[0])
        arrived = [from_inner(picked[k], k) for k in range(1, n_in)]
        pieces.extend(arrived)

    mine = local_stats([after(shard[k], done) for k in range(n_out)], near)
    mine = (mine[0], mine[1])
    count = tok_dev * n_out
    k = 1
    while k < n_in:
        other = from_inner(jnp.stack(mine), k)
        mine = merge(mine, (other[0], other[1]), count)
        count *= 2
        k *= 2
    product = gram(n_col, pair_count, slot_tile, pieces, near)
    return (product, mine[0] / total_tokens, mine[1] / total_tokens)


def plan_kernel(block_count, slot_ref, tile_ref, shard, plan, near_shard):
    col = lax.axis_index("col")
    mine = tile_ref[lax.axis_index("tok") * 2 + col]
    packed = jnp.where(mine < block_count * (block_count + 1) // 2, 1 << 24, 0)
    shift = 0
    for tile in (mine, tile_ref[lax.axis_index("tok") * 2 + 1 - col]):
        for member in pair_of(tile, block_count):
            packed += slot_ref[member] << shift
            shift += 6
    plan[...] = jnp.full((8, 128), packed, jnp.int32)
    near_shard[...] = shard[...]


def make_plan(block_count, block_slot, slot_tile, shard):
    near = Near(True)
    return pl.pallas_call(
        lambda *refs: plan_kernel(block_count, *refs),
        out_shape=[near.out((8, 128), jnp.int32), near.out(shard.shape, shard.dtype)],
        in_specs=[SMEM, SMEM, VMEM],
        out_specs=[VMEM, VMEM],
        compiler_params=pltpu.CompilerParams(vmem_limit_bytes=2 << 20),
        name="plan",
    )(hbm(block_slot), hbm(slot_tile), hbm(shard))


def hbm(a):
    return pltpu.with_memory_space_constraint(a, pltpu.HBM)


def planned(plan):
    packed = jnp.max(plan[0:1, :])
    blocks = [(packed >> (6 * k)) & 63 for k in range(4)]
    return blocks[:2], blocks[2:], packed >= 1 << 24


def stat_tree(parts, count):
    while len(parts) > 1:
        half = len(parts) // 2
        parts = [merge(parts[k], parts[k + half], count) for k in range(half)]
        count *= 2
    return parts[0]


def shard_stats(ref):
    values = ref[...].astype(jnp.float32)
    part = jnp.sum(values, axis=0, keepdims=True)
    mean = part / values.shape[0]
    return part, jnp.sum((values - mean) ** 2, axis=0, keepdims=True)


def take_block(block, col, held, pieces, starts, dst):
    owner = lax.div(block, held)
    column = pl.multiple_of((block - owner * held) * BS, BS)

    @pl.when(owner == col)
    def _():
        for ref, start in zip(pieces, starts):
            dst[pl.ds(start, ref.shape[0]), :] = ref[:, pl.ds(column, BS)]


def wave_kernel(sizes, plan, *refs):
    arrays, (own, other, stats) = refs[:-3], refs[-3:]
    tok_dev, width = arrays[0].shape
    col = lax.axis_index("col")
    places = (0, 1 + col, 2 - col, 3)
    starts, done, row = [], 0, 0
    for size in sizes:
        starts += [pl.multiple_of((done + p) * tok_dev, tok_dev) for p in places[:size]]
        parts = [shard_stats(ref) for ref in arrays[done : done + size]]
        if size == 4:
            parts = [stat_tree(parts, tok_dev)]
        else:
            parts = [merge(parts[0], parts[2], tok_dev), parts[1]]
        for part, square in parts:
            stats[row : row + 1, :] = part
            stats[row + 1 : row + 2, :] = square
            row += 2
        done += size
    mine, theirs, _ = planned(plan)
    for out, blocks in ((own, mine), (other, theirs)):
        for side, block in enumerate(blocks):
            side_out = out.at[:, side * BS : (side + 1) * BS]
            take_block(block, col, width // BS, arrays, starts, side_out)


def wave_parts(plan, *waves):
    near = Near(True)
    shards = [a for wave in waves for a in wave]
    sizes = [len(wave) for wave in waves]
    tok_dev, width = shards[0].shape
    rows = len(shards) * tok_dev
    return pl.pallas_call(
        lambda *refs: wave_kernel(sizes, *refs),
        out_shape=[
            near.out((rows, 2 * BS), jnp.bfloat16),
            near.out((rows, 2 * BS), jnp.bfloat16),
            near.out((sum(2 if size == 4 else 4 for size in sizes), width), jnp.float32),
        ],
        in_specs=[VMEM] * (1 + len(shards)),
        out_specs=[VMEM] * 3,
        cost_estimate=pl.CostEstimate(flops=0, transcendentals=0, bytes_accessed=2 * rows * width),
        compiler_params=pltpu.CompilerParams(vmem_limit_bytes=4 << 20),
        name="wave",
    )(near.put(plan), *[near.put(a) for a in shards])


def assemble(blocks, col, held, own, other, sides, start):
    for side, block in enumerate(blocks):
        here = lax.div(block, held) == col
        for parts, taken in ((own, here), (other, jnp.logical_not(here))):

            @pl.when(taken)
            def _():
                row = start
                for ref in parts:
                    rows = ref.shape[0]
                    sides[side][row : row + rows, :] = ref[:, side * BS : (side + 1) * BS]
                    row += rows
    return start + sum(ref.shape[0] for ref in own)


def product_rows(left, right, m, rows):
    return lax.dot_general(
        left[:, m * rows : (m + 1) * rows],
        right[...],
        (((0,), (0,)), ((), ())),
        preferred_element_type=jnp.float32,
    )


def partial_kernel(held, plan, *refs):
    parts, (acc, left, right) = refs[:-3], refs[-3:]
    half = len(parts) // 2
    col = lax.axis_index("col")
    blocks = planned(plan)[0]
    assemble(blocks, col, held, parts[:half], parts[half:], (left, right), 0)
    rows = BS // 4
    for m in range(BS // rows):
        acc[m * rows : (m + 1) * rows, :] = product_rows(left, right, m, rows)


def partial_gram(held, plan, own, other):
    near = Near(True)
    tokens = sum(a.shape[0] for a in own)
    arrays = [near.put(a) for a in (plan, *own, *other)]
    return pl.pallas_call(
        lambda *refs: partial_kernel(held, *refs),
        out_shape=near.out((BS, BS), jnp.float32),
        in_specs=[VMEM] * len(arrays),
        out_specs=VMEM,
        scratch_shapes=[
            pltpu.VMEM((tokens, BS), jnp.bfloat16),
            pltpu.VMEM((tokens, BS), jnp.bfloat16),
        ],
        cost_estimate=pl.CostEstimate(
            flops=2 * tokens * BS * BS, transcendentals=0, bytes_accessed=0
        ),
        compiler_params=pltpu.CompilerParams(vmem_limit_bytes=8 << 20),
        name="partial",
    )(*arrays)


def finish_kernel(total_tokens, n_parts, plan, acc, *refs):
    own, other = refs[:n_parts], refs[n_parts : 2 * n_parts]
    far, far_other, *stats = refs[2 * n_parts : -8]
    out, mean, var, left, right, result, moments, sems = refs[-8:]
    tok_dev, width = far.shape
    held = width // BS
    col = lax.axis_index("col")
    blocks, _, live = planned(plan)
    start = assemble(blocks, col, held, own, other, (left, right), 0)
    for side, block in enumerate(blocks):
        for ref, half in ((far, col), (far_other, 1 - col)):
            take_block(block, half, held, [ref], [start], (left, right)[side])
    chunks = sems.shape[0] - 2
    rows = BS // chunks
    copies = []
    for m in range(chunks):
        here = slice(m * rows, (m + 1) * rows)
        total = acc[here, :] + product_rows(left, right, m, rows)
        result[here, :] = jnp.where(live, total / total_tokens, 0.0)
        copies.append(
            pltpu.make_async_copy(result.at[here, :], out.at[0, here, :], sems.at[m])
        )
        copies[-1].start()
    *whole, split, rest = [
        (ref[k : k + 1, :], ref[k + 1 : k + 2, :]) for ref in stats for k in range(0, ref.shape[0], 2)
    ]
    parts = [*whole, merge(split, merge(rest, shard_stats(far), tok_dev), 2 * tok_dev)]
    part, square = stat_tree(parts, 4 * tok_dev)
    for k, (ref, value) in enumerate(((mean, part), (var, square))):
        moments[k] = value / total_tokens
        copies.append(pltpu.make_async_copy(moments.at[k], ref, sems.at[chunks + k]))
        copies[-1].start()
    for copy in copies:
        copy.wait()


def finish(total_tokens, plan, acc, own, other, far, far_other, stats):
    near = Near(True)
    width = far.shape[1]
    tokens = sum(a.shape[0] for a in own) + far.shape[0]
    arrays = [near.put(a) for a in (plan, acc, *own, *other, far, far_other, *stats)]
    product, mean, var = pl.pallas_call(
        lambda *refs: finish_kernel(total_tokens, len(own), *refs),
        out_shape=[
            jax.ShapeDtypeStruct((1, BS, BS), jnp.float32),
            jax.ShapeDtypeStruct((1, width), jnp.float32),
            jax.ShapeDtypeStruct((1, width), jnp.float32),
        ],
        in_specs=[VMEM] * len(arrays),
        out_specs=[pl.BlockSpec(memory_space=pl.ANY)] * 3,
        scratch_shapes=[
            pltpu.VMEM((tokens, BS), jnp.bfloat16),
            pltpu.VMEM((tokens, BS), jnp.bfloat16),
            pltpu.VMEM((BS, BS), jnp.float32),
            pltpu.VMEM((2, 1, width), jnp.float32),
            pltpu.SemaphoreType.DMA((10,)),
        ],
        cost_estimate=pl.CostEstimate(
            flops=2 * tokens * BS * BS, transcendentals=0, bytes_accessed=4 * BS * BS
        ),
        compiler_params=pltpu.CompilerParams(vmem_limit_bytes=16 << 20),
        name="finish",
    )(*arrays)
    return product, mean[0], var[0]


def by_halves(activations, block_slot, slot_tile):
    n_tok = lax.axis_size("tok")
    tok_dev, width = activations.shape
    held = width // BS
    block_count = held * 2
    plan, own_shard = make_plan(block_count, block_slot, slot_tile, activations)

    def from_outer(a, k):
        return lax.ppermute(a, "tok", [(t, t ^ (4 * k)) for t in range(n_tok)])

    def from_plane(a, first):
        pairs = [
            (t * 2 + c, (t ^ (1 if (c == 0) == first else 2)) * 2 + c)
            for t in range(n_tok)
            for c in range(2)
        ]
        return lax.ppermute(a, ("tok", "col"), pairs)

    def from_sibling(a):
        return lax.ppermute(a, "col", [(0, 1), (1, 0)])

    z1 = from_outer(activations, 1)
    z2 = from_outer(activations, 2)
    s0 = from_plane(activations, True)
    z3 = from_outer(after(activations, s0), 3)
    b0 = from_plane(after(activations, s0), False)
    f0 = from_plane(after(s0, plan), False)
    s1 = from_plane(z1, True)
    b1 = from_plane(after(z1, z2), False)
    f1 = from_plane(after(s1, b0, f0, z2), False)
    s2 = from_plane(z2, True)
    b2 = from_plane(after(z2, b1), False)
    s3 = from_plane(z3, True)
    b3 = from_plane(z3, False)
    f3 = from_plane(after(s3, b1, b2), False)
    own0, out0, stats0 = wave_parts(plan, [own_shard, s0, b0, after(f0, s1)])
    f2 = from_plane(after(s2, f1, b1, z3, own0), False)
    other0 = from_sibling(out0)
    own1, out1, stats1 = wave_parts(plan, [z1, s1, b1, after(f1, f1)])
    other1 = from_sibling(out1)
    own2, out2, stats2 = wave_parts(plan, [z2, s2, b2, f2])
    other2 = from_sibling(out2)
    own3, out3, stats3 = wave_parts(plan, [z3, s3, after(b3, f2)])
    other3 = from_sibling(out3)
    acc = partial_gram(held, plan, [own0, own1], [other0, other1])
    far_other = from_sibling(f3)
    return finish(
        n_tok * tok_dev,
        plan,
        acc,
        [own2, own3],
        [other2, other3],
        f3,
        far_other,
        [stats0, stats1, stats2, stats3],
    )


def on_device(activations, block_slot, slot_tile):
    n_in = split_tok(lax.axis_size("tok"))[1]
    small = lax.axis_size("col") == 2 and lax.axis_size("tok") == 16
    return (by_halves if small else by_blocks)(activations, block_slot, slot_tile)


def solution(mesh):
    return jax.shard_map(
        on_device,
        mesh=mesh,
        in_specs=(P("tok", "col"), P(), P()),
        out_specs=(P(("tok", "col"), None, None), P("col"), P("col")),
        check_vma=False,
    )
```

```python
import jax
import jax.numpy as jnp
import numpy as np
from jax import lax
from jax.experimental import pallas as pl
from jax.experimental.pallas import tpu as pltpu
from jax.sharding import PartitionSpec as P

BS = 1024


def split_tok(n_tok):
    n_in = 1
    while n_in * n_in < n_tok:
        n_in *= 2
    return n_tok // n_in, n_in


def outer_waves(n_out):
    waves = [[0], [1, 2], [3]] if n_out >= 4 else [[k] for k in range(n_out)]
    return waves + [[k, k + 1] for k in range(4, n_out, 2)]


def pair_of(tile, block_count):
    pair_count = block_count * (block_count + 1) // 2
    tile = jnp.where(tile < pair_count, tile, 0)
    row = jnp.int32(0)
    start = jnp.int32(0)
    for r in range(1, block_count):
        first = r * block_count - r * (r - 1) // 2
        beyond = tile >= first
        row = jnp.where(beyond, r, row)
        start = jnp.where(beyond, first, start)
    return row, tile - start + row


def select_kernel(n_in, n_col, block_count, n_shards, *refs):
    slot_ref, tile_ref = refs[0], refs[1]
    shards = refs[2 : 2 + n_shards * n_col]
    outs = refs[2 + n_shards * n_col :]
    tok_dev, width = shards[0].shape
    held = width // BS
    tok = lax.axis_index("tok")
    col = lax.axis_index("col")
    inner = lax.rem(tok, n_in)
    for k in range(n_in):
        peer = tok - inner + (inner ^ k)
        pair = pair_of(tile_ref[peer * n_col + col], block_count)
        for side in range(2):
            block = slot_ref[pair[side]]
            owner = lax.div(block, held)
            column = pl.multiple_of((block - owner * held) * BS, BS)
            away = lax.rem(owner - col + n_col, n_col)
            for r in range(n_col):

                @pl.when(away == r)
                def _():
                    for s in range(n_shards):
                        outs[k][s * tok_dev : (s + 1) * tok_dev, side * BS : (side + 1) * BS] = (
                            shards[s * n_col + r][:, pl.ds(column, BS)]
                        )


def select(n_in, n_col, block_count, block_slot, slot_tile, shards, near):
    rows = len(shards) * shards[0][0].shape[0]
    flat = [near.put(a) for shard in shards for a in shard]
    return pl.pallas_call(
        lambda *refs: select_kernel(n_in, n_col, block_count, len(shards), *refs),
        out_shape=[near.out((rows, 2 * BS), jnp.bfloat16)] * n_in,
        in_specs=[SMEM, SMEM] + [VMEM] * len(flat),
        out_specs=[VMEM] * n_in,
        cost_estimate=pl.CostEstimate(flops=0, transcendentals=0, bytes_accessed=8 * rows * 2 * BS),
        name="select",
    )(block_slot, slot_tile, *flat)


def merge(a, b, count):
    return a[0] + b[0], a[1] + b[1] + (a[0] - b[0]) ** 2 / (2 * count)


def stats_kernel(*refs):
    shards, out = refs[:-1], refs[-1]
    count = shards[0].shape[0]
    parts = []
    for ref in shards:
        values = ref[...].astype(jnp.float32)
        part = jnp.sum(values, axis=0, keepdims=True)
        parts.append((part, jnp.sum((values - part / count) ** 2, axis=0, keepdims=True)))
    while len(parts) > 1:
        half = len(parts) // 2
        parts = [merge(parts[k], parts[k + half], count) for k in range(half)]
        count *= 2
    out[0:1, :] = parts[0][0]
    out[1:2, :] = parts[0][1]


def local_stats(shards, near):
    tok_dev, width = shards[0].shape
    return pl.pallas_call(
        stats_kernel,
        out_shape=near.out((2, width), jnp.float32),
        in_specs=[VMEM] * len(shards),
        out_specs=VMEM,
        cost_estimate=pl.CostEstimate(
            flops=4 * len(shards) * tok_dev * width,
            transcendentals=0,
            bytes_accessed=2 * len(shards) * tok_dev * width,
        ),
        name="stats",
    )(*[near.put(a) for a in shards])


def gram_kernel(n_col, pair_count, tile_ref, *refs):
    pieces, (out, left, right, chunk, sems) = refs[:-5], refs[-5:]
    total_tokens = left.shape[0]
    start = 0
    for ref in pieces:
        rows = ref.shape[0]
        left[start : start + rows, :] = ref[:, :BS]
        right[start : start + rows, :] = ref[:, BS:]
        start += rows
    mine = tile_ref[lax.axis_index("tok") * n_col + lax.axis_index("col")]
    rows = chunk.shape[1]
    copies = [None, None]
    for m in range(BS // rows):
        slot = m % 2
        if copies[slot] is not None:
            copies[slot].wait()
        product = lax.dot_general(
            left[:, m * rows : (m + 1) * rows],
            right[...],
            (((0,), (0,)), ((), ())),
            preferred_element_type=jnp.float32,
        )
        chunk[slot] = jnp.where(mine < pair_count, product / total_tokens, 0.0)
        copies[slot] = pltpu.make_async_copy(
            chunk.at[slot], out.at[0, m * rows : (m + 1) * rows, :], sems.at[slot]
        )
        copies[slot].start()
    for copy in copies:
        copy.wait()


def gram(n_col, pair_count, slot_tile, pieces, near):
    total_tokens = sum(a.shape[0] for a in pieces)
    return pl.pallas_call(
        lambda *refs: gram_kernel(n_col, pair_count, *refs),
        out_shape=jax.ShapeDtypeStruct((1, BS, BS), jnp.float32),
        in_specs=[SMEM] + [VMEM] * len(pieces),
        out_specs=pl.BlockSpec(memory_space=pl.ANY),
        scratch_shapes=[
            pltpu.VMEM((total_tokens, BS), jnp.bfloat16),
            pltpu.VMEM((total_tokens, BS), jnp.bfloat16),
            pltpu.VMEM((2, BS // 4, BS), jnp.float32),
            pltpu.SemaphoreType.DMA((2,)),
        ],
        cost_estimate=pl.CostEstimate(
            flops=2 * total_tokens * BS * BS, transcendentals=0, bytes_accessed=4 * BS * BS
        ),
        name="gram",
    )(slot_tile, *[near.put(a) for a in pieces])


SMEM = pl.BlockSpec(memory_space=pltpu.SMEM)
VMEM = pl.BlockSpec(memory_space=pltpu.VMEM)


class Near:
    def __init__(self, fits):
        self.fits = fits

    def put(self, a):
        return pltpu.with_memory_space_constraint(a, pltpu.VMEM) if self.fits else a

    def out(self, shape, dtype):
        return pltpu.VMEM(shape, dtype) if self.fits else jax.ShapeDtypeStruct(shape, dtype)


def after(value, *earlier):
    return lax.optimization_barrier((value, *earlier))[0]


def by_blocks(activations, block_slot, slot_tile):
    n_tok = lax.axis_size("tok")
    n_col = lax.axis_size("col")
    n_out, n_in = split_tok(n_tok)
    tok_dev, width = activations.shape
    total_tokens = tok_dev * n_tok
    block_count = width * n_col // BS
    pair_count = block_count * (block_count + 1) // 2
    held = 2 * tok_dev * (n_out * n_col * width + 2 * n_tok * 2 * BS)
    near = Near(held <= 12 << 20)

    def from_outer(a, k):
        return lax.ppermute(a, "tok", [(t, t ^ (k * n_in)) for t in range(n_tok)])

    def from_inner(a, k):
        return lax.ppermute(a, "tok", [(t, t ^ k) for t in range(n_tok)])

    def all_columns(a):
        return [a] + [
            lax.ppermute(a, "col", [(c, (c - r) % n_col) for c in range(n_col)])
            for r in range(1, n_col)
        ]

    waves = outer_waves(n_out)
    shard = {0: activations}
    source = activations
    pieces = []
    done = None
    for w, wave in enumerate(waves):
        full = []
        for k in wave:
            if k:
                shard[k] = after(from_outer(activations if w < 2 else source, k), done)
            full.append(all_columns(shard[k]))
        source = after(activations, *[shard[k] for k in wave if k])
        picked = select(n_in, n_col, block_count, block_slot, slot_tile, full, near)
        if pieces:
            picked = lax.optimization_barrier((*picked, *arrived))[:n_in]
        done = picked[0]
        pieces.append(picked[0])
        arrived = [from_inner(picked[k], k) for k in range(1, n_in)]
        pieces.extend(arrived)

    mine = local_stats([after(shard[k], done) for k in range(n_out)], near)
    mine = (mine[0], mine[1])
    count = tok_dev * n_out
    k = 1
    while k < n_in:
        other = from_inner(jnp.stack(mine), k)
        mine = merge(mine, (other[0], other[1]), count)
        count *= 2
        k *= 2
    product = gram(n_col, pair_count, slot_tile, pieces, near)
    return (product, mine[0] / total_tokens, mine[1] / total_tokens)


def plan_kernel(block_count, slot_ref, tile_ref, shard, plan, near_shard):
    col = lax.axis_index("col")
    mine = tile_ref[lax.axis_index("tok") * 2 + col]
    packed = jnp.where(mine < block_count * (block_count + 1) // 2, 1 << 24, 0)
    shift = 0
    for tile in (mine, tile_ref[lax.axis_index("tok") * 2 + 1 - col]):
        for member in pair_of(tile, block_count):
            packed += slot_ref[member] << shift
            shift += 6
    plan[...] = jnp.full((8, 128), packed, jnp.int32)
    near_shard[...] = shard[...]


def make_plan(block_count, block_slot, slot_tile, shard):
    near = Near(True)
    return pl.pallas_call(
        lambda *refs: plan_kernel(block_count, *refs),
        out_shape=[near.out((8, 128), jnp.int32), near.out(shard.shape, shard.dtype)],
        in_specs=[SMEM, SMEM, VMEM],
        out_specs=[VMEM, VMEM],
        compiler_params=pltpu.CompilerParams(vmem_limit_bytes=2 << 20),
        name="plan",
    )(hbm(block_slot), hbm(slot_tile), hbm(shard))


def hbm(a):
    return pltpu.with_memory_space_constraint(a, pltpu.HBM)


def planned(plan):
    packed = jnp.max(plan[0:1, :])
    blocks = [(packed >> (6 * k)) & 63 for k in range(4)]
    return blocks[:2], blocks[2:], packed >= 1 << 24


def stat_tree(parts, count):
    while len(parts) > 1:
        half = len(parts) // 2
        parts = [merge(parts[k], parts[k + half], count) for k in range(half)]
        count *= 2
    return parts[0]


def shard_stats(ref):
    values = ref[...].astype(jnp.float32)
    part = jnp.sum(values, axis=0, keepdims=True)
    mean = part / values.shape[0]
    return part, jnp.sum((values - mean) ** 2, axis=0, keepdims=True)


def take_block(block, col, held, pieces, starts, dst):
    owner = lax.div(block, held)
    column = pl.multiple_of((block - owner * held) * BS, BS)

    @pl.when(owner == col)
    def _():
        for ref, start in zip(pieces, starts):
            dst[pl.ds(start, ref.shape[0]), :] = ref[:, pl.ds(column, BS)]


def wave_kernel(sizes, plan, *refs):
    arrays, (own, other, stats) = refs[:-3], refs[-3:]
    tok_dev, width = arrays[0].shape
    col = lax.axis_index("col")
    places = (0, 1 + col, 2 - col, 3)
    starts, done, row = [], 0, 0
    for size in sizes:
        starts += [pl.multiple_of((done + p) * tok_dev, tok_dev) for p in places[:size]]
        parts = [shard_stats(ref) for ref in arrays[done : done + size]]
        if size == 4:
            parts = [stat_tree(parts, tok_dev)]
        else:
            parts = [merge(parts[0], parts[2], tok_dev), parts[1]]
        for part, square in parts:
            stats[row : row + 1, :] = part
            stats[row + 1 : row + 2, :] = square
            row += 2
        done += size
    mine, theirs, _ = planned(plan)
    for out, blocks in ((own, mine), (other, theirs)):
        for side, block in enumerate(blocks):
            side_out = out.at[:, side * BS : (side + 1) * BS]
            take_block(block, col, width // BS, arrays, starts, side_out)


def wave_parts(plan, *waves):
    near = Near(True)
    shards = [a for wave in waves for a in wave]
    sizes = [len(wave) for wave in waves]
    tok_dev, width = shards[0].shape
    rows = len(shards) * tok_dev
    return pl.pallas_call(
        lambda *refs: wave_kernel(sizes, *refs),
        out_shape=[
            near.out((rows, 2 * BS), jnp.bfloat16),
            near.out((rows, 2 * BS), jnp.bfloat16),
            near.out((sum(2 if size == 4 else 4 for size in sizes), width), jnp.float32),
        ],
        in_specs=[VMEM] * (1 + len(shards)),
        out_specs=[VMEM] * 3,
        cost_estimate=pl.CostEstimate(flops=0, transcendentals=0, bytes_accessed=2 * rows * width),
        compiler_params=pltpu.CompilerParams(vmem_limit_bytes=4 << 20),
        name="wave",
    )(near.put(plan), *[near.put(a) for a in shards])


def assemble(blocks, col, held, own, other, sides, start):
    for side, block in enumerate(blocks):
        here = lax.div(block, held) == col
        for parts, taken in ((own, here), (other, jnp.logical_not(here))):

            @pl.when(taken)
            def _():
                row = start
                for ref in parts:
                    rows = ref.shape[0]
                    sides[side][row : row + rows, :] = ref[:, side * BS : (side + 1) * BS]
                    row += rows
    return start + sum(ref.shape[0] for ref in own)


def product_rows(left, right, m, rows):
    return lax.dot_general(
        left[:, m * rows : (m + 1) * rows],
        right[...],
        (((0,), (0,)), ((), ())),
        preferred_element_type=jnp.float32,
    )


def partial_kernel(held, plan, *refs):
    parts, (acc, left, right) = refs[:-3], refs[-3:]
    half = len(parts) // 2
    col = lax.axis_index("col")
    blocks = planned(plan)[0]
    assemble(blocks, col, held, parts[:half], parts[half:], (left, right), 0)
    rows = BS // 4
    for m in range(BS // rows):
        acc[m * rows : (m + 1) * rows, :] = product_rows(left, right, m, rows)


def partial_gram(held, plan, own, other):
    near = Near(True)
    tokens = sum(a.shape[0] for a in own)
    arrays = [near.put(a) for a in (plan, *own, *other)]
    return pl.pallas_call(
        lambda *refs: partial_kernel(held, *refs),
        out_shape=near.out((BS, BS), jnp.float32),
        in_specs=[VMEM] * len(arrays),
        out_specs=VMEM,
        scratch_shapes=[
            pltpu.VMEM((tokens, BS), jnp.bfloat16),
            pltpu.VMEM((tokens, BS), jnp.bfloat16),
        ],
        cost_estimate=pl.CostEstimate(
            flops=2 * tokens * BS * BS, transcendentals=0, bytes_accessed=0
        ),
        compiler_params=pltpu.CompilerParams(vmem_limit_bytes=8 << 20),
        name="partial",
    )(*arrays)


def mean_over(total, count):
    return total * (1.0 / count) if count & (count - 1) == 0 else total / count


def finish_kernel(total_tokens, n_parts, plan, acc, *refs):
    own, other = refs[:n_parts], refs[n_parts : 2 * n_parts]
    far, far_other, *stats = refs[2 * n_parts : -8]
    out, mean, var, left, right, result, moments, sems = refs[-8:]
    tok_dev, width = far.shape
    held = width // BS
    col = lax.axis_index("col")
    blocks, _, live = planned(plan)
    start = assemble(blocks, col, held, own, other, (left, right), 0)
    for side, block in enumerate(blocks):
        for ref, half in ((far, col), (far_other, 1 - col)):
            take_block(block, half, held, [ref], [start], (left, right)[side])
    chunks = sems.shape[0] - 2
    rows = BS // chunks
    copies = []
    for m in range(chunks):
        here = slice(m * rows, (m + 1) * rows)
        total = acc[here, :] + product_rows(left, right, m, rows)
        result[here, :] = jnp.where(live, mean_over(total, total_tokens), 0.0)
        copies.append(
            pltpu.make_async_copy(result.at[here, :], out.at[0, here, :], sems.at[m])
        )
        copies[-1].start()
    *whole, split, rest = [
        (ref[k : k + 1, :], ref[k + 1 : k + 2, :]) for ref in stats for k in range(0, ref.shape[0], 2)
    ]
    parts = [*whole, merge(split, merge(rest, shard_stats(far), tok_dev), 2 * tok_dev)]
    part, square = stat_tree(parts, 4 * tok_dev)
    for k, (ref, value) in enumerate(((mean, part), (var, square))):
        moments[k] = value / total_tokens
        copies.append(pltpu.make_async_copy(moments.at[k], ref, sems.at[chunks + k]))
        copies[-1].start()
    for copy in copies:
        copy.wait()


def finish(total_tokens, plan, acc, own, other, far, far_other, stats):
    near = Near(True)
    width = far.shape[1]
    tokens = sum(a.shape[0] for a in own) + far.shape[0]
    arrays = [near.put(a) for a in (plan, acc, *own, *other, far, far_other, *stats)]
    product, mean, var = pl.pallas_call(
        lambda *refs: finish_kernel(total_tokens, len(own), *refs),
        out_shape=[
            jax.ShapeDtypeStruct((1, BS, BS), jnp.float32),
            jax.ShapeDtypeStruct((1, width), jnp.float32),
            jax.ShapeDtypeStruct((1, width), jnp.float32),
        ],
        in_specs=[VMEM] * len(arrays),
        out_specs=[pl.BlockSpec(memory_space=pl.ANY)] * 3,
        scratch_shapes=[
            pltpu.VMEM((tokens, BS), jnp.bfloat16),
            pltpu.VMEM((tokens, BS), jnp.bfloat16),
            pltpu.VMEM((BS, BS), jnp.float32),
            pltpu.VMEM((2, 1, width), jnp.float32),
            pltpu.SemaphoreType.DMA((10,)),
        ],
        cost_estimate=pl.CostEstimate(
            flops=2 * tokens * BS * BS, transcendentals=0, bytes_accessed=4 * BS * BS
        ),
        compiler_params=pltpu.CompilerParams(vmem_limit_bytes=16 << 20),
        name="finish",
    )(*arrays)
    return product, mean[0], var[0]


def by_halves(activations, block_slot, slot_tile):
    n_tok = lax.axis_size("tok")
    tok_dev, width = activations.shape
    held = width // BS
    block_count = held * 2
    plan, own_shard = make_plan(block_count, block_slot, slot_tile, activations)

    def from_outer(a, k):
        return lax.ppermute(a, "tok", [(t, t ^ (4 * k)) for t in range(n_tok)])

    def from_plane(a, first):
        pairs = [
            (t * 2 + c, (t ^ (1 if (c == 0) == first else 2)) * 2 + c)
            for t in range(n_tok)
            for c in range(2)
        ]
        return lax.ppermute(a, ("tok", "col"), pairs)

    def from_sibling(a):
        return lax.ppermute(a, "col", [(0, 1), (1, 0)])

    z1 = from_outer(activations, 1)
    z2 = from_outer(activations, 2)
    s0 = from_plane(activations, True)
    z3 = from_outer(after(activations, s0), 3)
    b0 = from_plane(after(activations, s0), False)
    f0 = from_plane(after(s0, plan), False)
    s1 = from_plane(z1, True)
    b1 = from_plane(after(z1, z2), False)
    f1 = from_plane(after(s1, b0, f0, z2), False)
    s2 = from_plane(z2, True)
    b2 = from_plane(after(z2, b1), False)
    s3 = from_plane(z3, True)
    b3 = from_plane(z3, False)
    f3 = from_plane(after(s3, b1, b2), False)
    own0, out0, stats0 = wave_parts(plan, [own_shard, s0, b0, after(f0, s1)])
    f2 = from_plane(after(s2, f1, b1, z3, own0), False)
    other0 = from_sibling(out0)
    own1, out1, stats1 = wave_parts(plan, [z1, s1, b1, after(f1, f1)])
    other1 = from_sibling(out1)
    own2, out2, stats2 = wave_parts(plan, [z2, s2, b2, f2])
    other2 = from_sibling(out2)
    own3, out3, stats3 = wave_parts(plan, [z3, s3, after(b3, f2)])
    other3 = from_sibling(out3)
    acc = partial_gram(held, plan, [own0, own1], [other0, other1])
    far_other = from_sibling(f3)
    return finish(
        n_tok * tok_dev,
        plan,
        acc,
        [own2, own3],
        [other2, other3],
        f3,
        far_other,
        [stats0, stats1, stats2, stats3],
    )


def on_device(activations, block_slot, slot_tile):
    n_in = split_tok(lax.axis_size("tok"))[1]
    small = lax.axis_size("col") == 2 and lax.axis_size("tok") == 16
    return (by_halves if small else by_blocks)(activations, block_slot, slot_tile)


def solution(mesh):
    return jax.shard_map(
        on_device,
        mesh=mesh,
        in_specs=(P("tok", "col"), P(), P()),
        out_specs=(P(("tok", "col"), None, None), P("col"), P("col")),
        check_vma=False,
    )
```

```python
import jax
import jax.numpy as jnp
import numpy as np
from jax import lax
from jax.experimental import pallas as pl
from jax.experimental.pallas import tpu as pltpu
from jax.sharding import PartitionSpec as P

BS = 1024


def split_tok(n_tok):
    n_in = 1
    while n_in * n_in < n_tok:
        n_in *= 2
    return n_tok // n_in, n_in


def outer_waves(n_out):
    waves = [[0], [1, 2], [3]] if n_out >= 4 else [[k] for k in range(n_out)]
    return waves + [[k, k + 1] for k in range(4, n_out, 2)]


def pair_of(tile, block_count):
    pair_count = block_count * (block_count + 1) // 2
    tile = jnp.where(tile < pair_count, tile, 0)
    row = jnp.int32(0)
    start = jnp.int32(0)
    for r in range(1, block_count):
        first = r * block_count - r * (r - 1) // 2
        beyond = tile >= first
        row = jnp.where(beyond, r, row)
        start = jnp.where(beyond, first, start)
    return row, tile - start + row


def select_kernel(n_in, n_col, block_count, n_shards, *refs):
    slot_ref, tile_ref = refs[0], refs[1]
    shards = refs[2 : 2 + n_shards * n_col]
    outs = refs[2 + n_shards * n_col :]
    tok_dev, width = shards[0].shape
    held = width // BS
    tok = lax.axis_index("tok")
    col = lax.axis_index("col")
    inner = lax.rem(tok, n_in)
    for k in range(n_in):
        peer = tok - inner + (inner ^ k)
        pair = pair_of(tile_ref[peer * n_col + col], block_count)
        for side in range(2):
            block = slot_ref[pair[side]]
            owner = lax.div(block, held)
            column = pl.multiple_of((block - owner * held) * BS, BS)
            away = lax.rem(owner - col + n_col, n_col)
            for r in range(n_col):

                @pl.when(away == r)
                def _():
                    for s in range(n_shards):
                        outs[k][s * tok_dev : (s + 1) * tok_dev, side * BS : (side + 1) * BS] = (
                            shards[s * n_col + r][:, pl.ds(column, BS)]
                        )


def select(n_in, n_col, block_count, block_slot, slot_tile, shards, near):
    rows = len(shards) * shards[0][0].shape[0]
    flat = [near.put(a) for shard in shards for a in shard]
    return pl.pallas_call(
        lambda *refs: select_kernel(n_in, n_col, block_count, len(shards), *refs),
        out_shape=[near.out((rows, 2 * BS), jnp.bfloat16)] * n_in,
        in_specs=[SMEM, SMEM] + [VMEM] * len(flat),
        out_specs=[VMEM] * n_in,
        cost_estimate=pl.CostEstimate(flops=0, transcendentals=0, bytes_accessed=8 * rows * 2 * BS),
        name="select",
    )(block_slot, slot_tile, *flat)


def merge(a, b, count):
    return a[0] + b[0], a[1] + b[1] + (a[0] - b[0]) ** 2 / (2 * count)


def stats_kernel(*refs):
    shards, out = refs[:-1], refs[-1]
    count = shards[0].shape[0]
    parts = []
    for ref in shards:
        values = ref[...].astype(jnp.float32)
        part = jnp.sum(values, axis=0, keepdims=True)
        parts.append((part, jnp.sum((values - part / count) ** 2, axis=0, keepdims=True)))
    while len(parts) > 1:
        half = len(parts) // 2
        parts = [merge(parts[k], parts[k + half], count) for k in range(half)]
        count *= 2
    out[0:1, :] = parts[0][0]
    out[1:2, :] = parts[0][1]


def local_stats(shards, near):
    tok_dev, width = shards[0].shape
    return pl.pallas_call(
        stats_kernel,
        out_shape=near.out((2, width), jnp.float32),
        in_specs=[VMEM] * len(shards),
        out_specs=VMEM,
        cost_estimate=pl.CostEstimate(
            flops=4 * len(shards) * tok_dev * width,
            transcendentals=0,
            bytes_accessed=2 * len(shards) * tok_dev * width,
        ),
        name="stats",
    )(*[near.put(a) for a in shards])


def gram_kernel(n_col, pair_count, tile_ref, *refs):
    pieces, (out, left, right, chunk, sems) = refs[:-5], refs[-5:]
    total_tokens = left.shape[0]
    start = 0
    for ref in pieces:
        rows = ref.shape[0]
        left[start : start + rows, :] = ref[:, :BS]
        right[start : start + rows, :] = ref[:, BS:]
        start += rows
    mine = tile_ref[lax.axis_index("tok") * n_col + lax.axis_index("col")]
    rows = chunk.shape[1]
    copies = [None, None]
    for m in range(BS // rows):
        slot = m % 2
        if copies[slot] is not None:
            copies[slot].wait()
        product = lax.dot_general(
            left[:, m * rows : (m + 1) * rows],
            right[...],
            (((0,), (0,)), ((), ())),
            preferred_element_type=jnp.float32,
        )
        chunk[slot] = jnp.where(mine < pair_count, product / total_tokens, 0.0)
        copies[slot] = pltpu.make_async_copy(
            chunk.at[slot], out.at[0, m * rows : (m + 1) * rows, :], sems.at[slot]
        )
        copies[slot].start()
    for copy in copies:
        copy.wait()


def gram(n_col, pair_count, slot_tile, pieces, near):
    total_tokens = sum(a.shape[0] for a in pieces)
    return pl.pallas_call(
        lambda *refs: gram_kernel(n_col, pair_count, *refs),
        out_shape=jax.ShapeDtypeStruct((1, BS, BS), jnp.float32),
        in_specs=[SMEM] + [VMEM] * len(pieces),
        out_specs=pl.BlockSpec(memory_space=pl.ANY),
        scratch_shapes=[
            pltpu.VMEM((total_tokens, BS), jnp.bfloat16),
            pltpu.VMEM((total_tokens, BS), jnp.bfloat16),
            pltpu.VMEM((2, BS // 4, BS), jnp.float32),
            pltpu.SemaphoreType.DMA((2,)),
        ],
        cost_estimate=pl.CostEstimate(
            flops=2 * total_tokens * BS * BS, transcendentals=0, bytes_accessed=4 * BS * BS
        ),
        name="gram",
    )(slot_tile, *[near.put(a) for a in pieces])


SMEM = pl.BlockSpec(memory_space=pltpu.SMEM)
VMEM = pl.BlockSpec(memory_space=pltpu.VMEM)


class Near:
    def __init__(self, fits):
        self.fits = fits

    def put(self, a):
        return pltpu.with_memory_space_constraint(a, pltpu.VMEM) if self.fits else a

    def out(self, shape, dtype):
        return pltpu.VMEM(shape, dtype) if self.fits else jax.ShapeDtypeStruct(shape, dtype)


def after(value, *earlier):
    return lax.optimization_barrier((value, *earlier))[0]


def by_blocks(activations, block_slot, slot_tile):
    n_tok = lax.axis_size("tok")
    n_col = lax.axis_size("col")
    n_out, n_in = split_tok(n_tok)
    tok_dev, width = activations.shape
    total_tokens = tok_dev * n_tok
    block_count = width * n_col // BS
    pair_count = block_count * (block_count + 1) // 2
    held = 2 * tok_dev * (n_out * n_col * width + 2 * n_tok * 2 * BS)
    near = Near(held <= 12 << 20)

    def from_outer(a, k):
        return lax.ppermute(a, "tok", [(t, t ^ (k * n_in)) for t in range(n_tok)])

    def from_inner(a, k):
        return lax.ppermute(a, "tok", [(t, t ^ k) for t in range(n_tok)])

    def all_columns(a):
        return [a] + [
            lax.ppermute(a, "col", [(c, (c - r) % n_col) for c in range(n_col)])
            for r in range(1, n_col)
        ]

    waves = outer_waves(n_out)
    shard = {0: activations}
    source = activations
    pieces = []
    done = None
    for w, wave in enumerate(waves):
        full = []
        for k in wave:
            if k:
                shard[k] = after(from_outer(activations if w < 2 else source, k), done)
            full.append(all_columns(shard[k]))
        source = after(activations, *[shard[k] for k in wave if k])
        picked = select(n_in, n_col, block_count, block_slot, slot_tile, full, near)
        if pieces:
            picked = lax.optimization_barrier((*picked, *arrived))[:n_in]
        done = picked[0]
        pieces.append(picked[0])
        arrived = [from_inner(picked[k], k) for k in range(1, n_in)]
        pieces.extend(arrived)

    mine = local_stats([after(shard[k], done) for k in range(n_out)], near)
    mine = (mine[0], mine[1])
    count = tok_dev * n_out
    k = 1
    while k < n_in:
        other = from_inner(jnp.stack(mine), k)
        mine = merge(mine, (other[0], other[1]), count)
        count *= 2
        k *= 2
    product = gram(n_col, pair_count, slot_tile, pieces, near)
    return (product, mine[0] / total_tokens, mine[1] / total_tokens)


def plan_kernel(block_count, slot_ref, tile_ref, shard, plan, near_shard):
    col = lax.axis_index("col")
    mine = tile_ref[lax.axis_index("tok") * 2 + col]
    packed = jnp.where(mine < block_count * (block_count + 1) // 2, 1 << 24, 0)
    shift = 0
    for tile in (mine, tile_ref[lax.axis_index("tok") * 2 + 1 - col]):
        for member in pair_of(tile, block_count):
            packed += slot_ref[member] << shift
            shift += 6
    plan[...] = jnp.full((8, 128), packed, jnp.int32)
    near_shard[...] = shard[...]


def make_plan(block_count, block_slot, slot_tile, shard):
    near = Near(True)
    return pl.pallas_call(
        lambda *refs: plan_kernel(block_count, *refs),
        out_shape=[near.out((8, 128), jnp.int32), near.out(shard.shape, shard.dtype)],
        in_specs=[SMEM, SMEM, VMEM],
        out_specs=[VMEM, VMEM],
        compiler_params=pltpu.CompilerParams(vmem_limit_bytes=2 << 20),
        name="plan",
    )(hbm(block_slot), hbm(slot_tile), hbm(shard))


def hbm(a):
    return pltpu.with_memory_space_constraint(a, pltpu.HBM)


def planned(plan):
    packed = jnp.max(plan[0:1, :])
    blocks = [(packed >> (6 * k)) & 63 for k in range(4)]
    return blocks[:2], blocks[2:], packed >= 1 << 24


def stat_tree(parts, count):
    while len(parts) > 1:
        half = len(parts) // 2
        parts = [merge(parts[k], parts[k + half], count) for k in range(half)]
        count *= 2
    return parts[0]


def shard_stats(ref):
    values = ref[...].astype(jnp.float32)
    part = jnp.sum(values, axis=0, keepdims=True)
    mean = part / values.shape[0]
    return part, jnp.sum((values - mean) ** 2, axis=0, keepdims=True)


def take_block(block, col, held, pieces, starts, dst):
    owner = lax.div(block, held)
    column = pl.multiple_of((block - owner * held) * BS, BS)

    @pl.when(owner == col)
    def _():
        for ref, start in zip(pieces, starts):
            dst[pl.ds(start, ref.shape[0]), :] = ref[:, pl.ds(column, BS)]


def wave_kernel(sizes, plan, *refs):
    arrays, (own, other, stats) = refs[:-3], refs[-3:]
    tok_dev, width = arrays[0].shape
    col = lax.axis_index("col")
    places = (0, 1 + col, 2 - col, 3)
    starts, done, row = [], 0, 0
    for size in sizes:
        starts += [pl.multiple_of((done + p) * tok_dev, tok_dev) for p in places[:size]]
        parts = [shard_stats(ref) for ref in arrays[done : done + size]]
        if size == 4:
            parts = [stat_tree(parts, tok_dev)]
        else:
            parts = [merge(parts[0], parts[2], tok_dev), parts[1]]
        for part, square in parts:
            stats[row : row + 1, :] = part
            stats[row + 1 : row + 2, :] = square
            row += 2
        done += size
    mine, theirs, _ = planned(plan)
    for out, blocks in ((own, mine), (other, theirs)):
        for side, block in enumerate(blocks):
            side_out = out.at[:, side * BS : (side + 1) * BS]
            take_block(block, col, width // BS, arrays, starts, side_out)


def wave_parts(plan, *waves):
    near = Near(True)
    shards = [a for wave in waves for a in wave]
    sizes = [len(wave) for wave in waves]
    tok_dev, width = shards[0].shape
    rows = len(shards) * tok_dev
    return pl.pallas_call(
        lambda *refs: wave_kernel(sizes, *refs),
        out_shape=[
            near.out((rows, 2 * BS), jnp.bfloat16),
            near.out((rows, 2 * BS), jnp.bfloat16),
            near.out((sum(2 if size == 4 else 4 for size in sizes), width), jnp.float32),
        ],
        in_specs=[VMEM] * (1 + len(shards)),
        out_specs=[VMEM] * 3,
        cost_estimate=pl.CostEstimate(flops=0, transcendentals=0, bytes_accessed=2 * rows * width),
        compiler_params=pltpu.CompilerParams(vmem_limit_bytes=4 << 20),
        name="wave",
    )(near.put(plan), *[near.put(a) for a in shards])


def assemble(blocks, col, held, own, other, sides, start):
    for side, block in enumerate(blocks):
        here = lax.div(block, held) == col
        for parts, taken in ((own, here), (other, jnp.logical_not(here))):

            @pl.when(taken)
            def _():
                row = start
                for ref in parts:
                    rows = ref.shape[0]
                    sides[side][row : row + rows, :] = ref[:, side * BS : (side + 1) * BS]
                    row += rows
    return start + sum(ref.shape[0] for ref in own)


def product_rows(left, right, m, rows):
    return lax.dot_general(
        left[:, m * rows : (m + 1) * rows],
        right[...],
        (((0,), (0,)), ((), ())),
        preferred_element_type=jnp.float32,
    )


def partial_kernel(held, plan, *refs):
    parts, (acc, left, right) = refs[:-3], refs[-3:]
    half = len(parts) // 2
    col = lax.axis_index("col")
    blocks = planned(plan)[0]
    assemble(blocks, col, held, parts[:half], parts[half:], (left, right), 0)
    rows = BS // 4
    for m in range(BS // rows):
        acc[m * rows : (m + 1) * rows, :] = product_rows(left, right, m, rows)


def partial_gram(held, plan, own, other):
    near = Near(True)
    tokens = sum(a.shape[0] for a in own)
    arrays = [near.put(a) for a in (plan, *own, *other)]
    return pl.pallas_call(
        lambda *refs: partial_kernel(held, *refs),
        out_shape=near.out((BS, BS), jnp.float32),
        in_specs=[VMEM] * len(arrays),
        out_specs=VMEM,
        scratch_shapes=[
            pltpu.VMEM((tokens, BS), jnp.bfloat16),
            pltpu.VMEM((tokens, BS), jnp.bfloat16),
        ],
        cost_estimate=pl.CostEstimate(
            flops=2 * tokens * BS * BS, transcendentals=0, bytes_accessed=0
        ),
        compiler_params=pltpu.CompilerParams(vmem_limit_bytes=8 << 20),
        name="partial",
    )(*arrays)


def finish_kernel(total_tokens, n_parts, plan, acc, *refs):
    own, other = refs[:n_parts], refs[n_parts : 2 * n_parts]
    far, far_other, *stats = refs[2 * n_parts : -8]
    out, mean, var, left, right, result, moments, sems = refs[-8:]
    tok_dev, width = far.shape
    held = width // BS
    col = lax.axis_index("col")
    blocks, _, live = planned(plan)
    start = assemble(blocks, col, held, own, other, (left, right), 0)
    for side, block in enumerate(blocks):
        for ref, half in ((far, col), (far_other, 1 - col)):
            take_block(block, half, held, [ref], [start], (left, right)[side])
    chunks = sems.shape[0] - 2
    rows = BS // chunks
    copies = []
    for m in range(chunks):
        here = slice(m * rows, (m + 1) * rows)
        total = acc[here, :] + product_rows(left, right, m, rows)
        result[here, :] = jnp.where(live, total / total_tokens, 0.0)
        copies.append(
            pltpu.make_async_copy(result.at[here, :], out.at[0, here, :], sems.at[m])
        )
        copies[-1].start()
    *whole, split, rest = [
        (ref[k : k + 1, :], ref[k + 1 : k + 2, :]) for ref in stats for k in range(0, ref.shape[0], 2)
    ]
    parts = [*whole, merge(split, merge(rest, shard_stats(far), tok_dev), 2 * tok_dev)]
    part, square = stat_tree(parts, 4 * tok_dev)
    for k, (ref, value) in enumerate(((mean, part), (var, square))):
        moments[k] = value / total_tokens
        copies.append(pltpu.make_async_copy(moments.at[k], ref, sems.at[chunks + k]))
        copies[-1].start()
    for copy in copies:
        copy.wait()


def finish(total_tokens, plan, acc, own, other, far, far_other, stats):
    near = Near(True)
    width = far.shape[1]
    tokens = sum(a.shape[0] for a in own) + far.shape[0]
    arrays = [near.put(a) for a in (plan, acc, *own, *other, far, far_other, *stats)]
    product, mean, var = pl.pallas_call(
        lambda *refs: finish_kernel(total_tokens, len(own), *refs),
        out_shape=[
            jax.ShapeDtypeStruct((1, BS, BS), jnp.float32),
            jax.ShapeDtypeStruct((1, width), jnp.float32),
            jax.ShapeDtypeStruct((1, width), jnp.float32),
        ],
        in_specs=[VMEM] * len(arrays),
        out_specs=[pl.BlockSpec(memory_space=pl.ANY)] * 3,
        scratch_shapes=[
            pltpu.VMEM((tokens, BS), jnp.bfloat16),
            pltpu.VMEM((tokens, BS), jnp.bfloat16),
            pltpu.VMEM((BS, BS), jnp.float32),
            pltpu.VMEM((2, 1, width), jnp.float32),
            pltpu.SemaphoreType.DMA((10,)),
        ],
        cost_estimate=pl.CostEstimate(
            flops=2 * tokens * BS * BS, transcendentals=0, bytes_accessed=4 * BS * BS
        ),
        compiler_params=pltpu.CompilerParams(vmem_limit_bytes=16 << 20),
        name="finish",
    )(*arrays)
    return product, mean[0], var[0]


def by_halves(activations, block_slot, slot_tile):
    n_tok = lax.axis_size("tok")
    tok_dev, width = activations.shape
    held = width // BS
    block_count = held * 2
    plan, own_shard = make_plan(block_count, block_slot, slot_tile, activations)

    def from_outer(a, k):
        return lax.ppermute(a, "tok", [(t, t ^ (4 * k)) for t in range(n_tok)])

    def from_plane(a, first):
        pairs = [
            (t * 2 + c, (t ^ (1 if (c == 0) == first else 2)) * 2 + c)
            for t in range(n_tok)
            for c in range(2)
        ]
        return lax.ppermute(a, ("tok", "col"), pairs)

    def from_sibling(a):
        return lax.ppermute(a, "col", [(0, 1), (1, 0)])

    z1 = from_outer(activations, 1)
    z2 = from_outer(activations, 2)
    s0 = from_plane(activations, True)
    z3 = from_outer(after(activations, s0), 3)
    b0 = from_plane(after(activations, s0), False)
    f0 = from_plane(after(s0, plan), False)
    s1 = from_plane(z1, True)
    b1 = from_plane(after(z1, z2), False)
    f1 = from_plane(after(s1, b0, f0, z2), False)
    s2 = from_plane(z2, True)
    b2 = from_plane(after(z2, b1), False)
    s3 = from_plane(z3, True)
    b3 = from_plane(z3, False)
    own0, out0, stats0 = wave_parts(plan, [own_shard, s0, b0, after(f0, s1)])
    f2 = from_plane(after(s2, f1, b1, z3, own0), False)
    other0 = from_sibling(out0)
    own1, out1, stats1 = wave_parts(plan, [z1, s1, b1, after(f1, f1)])
    f3 = from_plane(after(s3, b1, b2, own1), False)
    other1 = from_sibling(out1)
    own2, out2, stats2 = wave_parts(plan, [z2, s2, b2, f2])
    other2 = from_sibling(out2)
    own3, out3, stats3 = wave_parts(plan, [z3, s3, after(b3, f2)])
    other3 = from_sibling(out3)
    acc = partial_gram(held, plan, [own0, own1], [other0, other1])
    far_other = from_sibling(f3)
    return finish(
        n_tok * tok_dev,
        plan,
        acc,
        [own2, own3],
        [other2, other3],
        f3,
        far_other,
        [stats0, stats1, stats2, stats3],
    )


def on_device(activations, block_slot, slot_tile):
    n_in = split_tok(lax.axis_size("tok"))[1]
    small = lax.axis_size("col") == 2 and lax.axis_size("tok") == 16
    return (by_halves if small else by_blocks)(activations, block_slot, slot_tile)


def solution(mesh):
    return jax.shard_map(
        on_device,
        mesh=mesh,
        in_specs=(P("tok", "col"), P(), P()),
        out_specs=(P(("tok", "col"), None, None), P("col"), P("col")),
        check_vma=False,
    )
```
